32 devices in a mesh: ctx: 8 (over z, y), mp: 4 (over x, core).
Axes of the slice: x: 2, y: 2, z: 4, core: 2. Of those that a mesh axis runs over, the one named last changes fastest.
Arguments:
- q_in: bfloat16 [8192, 4096], P('ctx', 'mp'), may hold values from -6 to 6
- k_in: bfloat16 [8192, 4096], P('ctx', 'mp'), may hold values from -6 to 6
- v_in: bfloat16 [8192, 4096], P('ctx', 'mp'), may hold values from -6 to 6
- short_filter: float32 [3, 7, 4096], P(None, None, 'mp'), may hold values from -2 to 2
- taps: float32 [128, 4096], P(None, 'mp'), may hold values from -0.5 to 0.5
- residue: float32 [16, 4096], P(None, 'mp'), may hold values from -3 to 3
- rate: float32 [16, 4096], P(None, 'mp'), may hold values from 2.3692846e-06 to 0.033333335
- out_weight: bfloat16 [4096, 4096], P('mp', 'ctx'), may hold values from -0.09375 to 0.09375
Outputs:
- mixed: bfloat16 [8192, 4096], P('ctx', 'mp')
The draws below stay inside these ranges and needn't reach their ends.
All inputs are finite; a program needn't handle non-finite values.
Results may differ from the reference program's by a relative error of at most 0.0095.
Values may be sent and summed in bfloat16 or wider, within the bound.
A program may use at most 192 MiB of HBM per device.

```python
import math
import jax
import jax.numpy as jnp
from jax import lax

D = 4096
TOK_DEV = 1024
MODES = 16
SHORT_LEN = 7
MEDIUM_LEN = 128
SEQ = 8192
N_MP = 4


def levels(rng, extent, cuts, least, top_value):
    def one(position, parts):
        draws = jax.random.uniform(jax.random.fold_in(jax.random.fold_in(rng, 6), position), (parts,), jnp.float32, least / len(cuts), top_value / len(cuts))
        return jnp.repeat(jnp.exp(draws), extent[position] // parts).reshape((-1,) + (1,) * (len(extent) - position - 1))

    level = one(*cuts[0])
    for cut in cuts[1:]:
        level = level * one(*cut)
    return level


def bell_draw(rng, dims, scale, reach, cuts=(), dtype=jnp.bfloat16):
    values = scale * jax.random.normal(rng, dims, jnp.float32)
    if cuts:
        values = values * levels(rng, dims, cuts, -0.22, 0.18)
    return jnp.clip(values, -reach, reach).astype(dtype)


def setup_inputs(seed: int = 0) -> dict:
    streams_of = jax.random.split(jax.random.key(seed), 9)
    q_in = bell_draw(streams_of[0], (SEQ, D), 1.0, 6.0, ((0, 8), (1, 4)))
    k_in = bell_draw(streams_of[1], (SEQ, D), 1.0, 6.0, ((0, 8), (1, 4)))
    v_in = bell_draw(streams_of[2], (SEQ, D), 1.0, 6.0, ((0, 8), (1, 4)))
    short_filter = bell_draw(streams_of[3], (3, SHORT_LEN, D), SHORT_LEN ** -0.5, 2.0, ((2, 4),), jnp.float32)
    taps = bell_draw(streams_of[4], (MEDIUM_LEN, D), 0.08, 0.5, ((1, 4),), jnp.float32)
    residue = bell_draw(streams_of[5], (MODES, D), 0.5, 3.0, ((1, 4),), jnp.float32)
    rate = jnp.clip(jnp.exp(math.log(0.033333335) - 9.551725 * jax.random.uniform(streams_of[6], (MODES, D), jnp.float32) ** levels(streams_of[6], (MODES, D), ((1, 4),), -0.2, 0.2)), 2.3692846298217773e-06, 0.033333335)
    out_weight = bell_draw(streams_of[7], (D, D), D ** -0.5, 0.09375, ((0, 4), (1, 8)))
    return dict(q_in=q_in, k_in=k_in, v_in=v_in, short_filter=short_filter, taps=taps, residue=residue, rate=rate, out_weight=out_weight)


def causal_short(signal, filt_rows):
    values = signal.astype(jnp.float32)
    padded = jnp.pad(values, ((SHORT_LEN - 1, 0), (0, 0)))
    running = jnp.zeros_like(values)
    for offset in range(SHORT_LEN):
        first_row = SHORT_LEN - 1 - offset
        running = running + filt_rows[offset][None, :] * padded[first_row:first_row + SEQ]
    return running

def long_group(packed):
    signal, tap_cols, rate_cols, mode_cols = packed
    moments = jnp.arange(SEQ).astype(jnp.float32)[:, None]
    kernel = jnp.zeros(signal.shape, jnp.float32)
    for mode_idx in range(MODES):
        kernel = kernel + mode_cols[mode_idx][None, :] * jnp.exp(-rate_cols[mode_idx][None, :] * moments)
    kernel = kernel.at[:MEDIUM_LEN].add(tap_cols)
    length = 2 * SEQ
    spectrum = jnp.fft.rfft(signal, n=length, axis=0) * jnp.fft.rfft(kernel, n=length, axis=0)
    return jnp.fft.irfft(spectrum, n=length, axis=0)[:SEQ].astype(jnp.float32)

def reference(q_in, k_in, v_in, short_filter, taps, residue, rate, out_weight):
    q_short = causal_short(q_in, short_filter[0]).astype(jnp.bfloat16)
    gated_sig = (causal_short(k_in, short_filter[1]) * causal_short(v_in, short_filter[2])).astype(jnp.bfloat16)
    mode_weight = residue * jnp.sqrt(2.0 * rate)
    chan_group = min(D, 256)
    group_count = D // chan_group

    def split_cols(matrix):
        return matrix.reshape(matrix.shape[0], group_count, chan_group).transpose(1, 0, 2)
    outputs = lax.map(long_group, (split_cols(gated_sig.astype(jnp.float32)), split_cols(taps), split_cols(rate), split_cols(mode_weight)))
    long_conv = outputs.transpose(1, 0, 2).reshape(SEQ, D).astype(jnp.bfloat16)
    product = (q_short.astype(jnp.float32) * long_conv.astype(jnp.float32)).astype(jnp.bfloat16)
    chan_share = D // N_MP

    def project(tok_block):
        summed = jnp.zeros((tok_block.shape[0], D), jnp.float32)
        for shard_idx in range(N_MP):
            lo_col = shard_idx * chan_share
            part_sum = jnp.dot(tok_block[:, lo_col:lo_col + chan_share], out_weight[lo_col:lo_col + chan_share], preferred_element_type=jnp.float32)
            rounded = lax.optimization_barrier(part_sum.astype(jnp.bfloat16))
            summed = summed + rounded.astype(jnp.float32)
        return summed.astype(jnp.bfloat16)
    mixed = lax.map(project, product.reshape(SEQ // TOK_DEV, TOK_DEV, D))
    return mixed.reshape(SEQ, D)
```

```python
import functools

import jax
import jax.numpy as jnp
import numpy as np
from jax import lax
from jax.experimental import pallas as pl
from jax.experimental.pallas import tpu as pltpu
from jax.sharding import PartitionSpec as P

SHORT_LEN = 7
LANES = 128
LEAD = 8


def shifted(array, axis):
    peers = lax.axis_size(axis)
    return lax.ppermute(array, axis, [(i, i + 1) for i in range(peers - 1)])


def split_const(matrix):
    high = matrix.astype(jnp.bfloat16)
    low = (matrix - high.astype(np.float64)).astype(jnp.bfloat16)
    return jnp.asarray(np.stack([high, low]))


@functools.lru_cache
def dft_matrices(block):
    size = 2 * block
    freq = np.arange(block)[:, None]
    pos = np.arange(block)[None, :]
    angle = 2 * np.pi * ((freq * pos) % size) / size
    fwd = np.concatenate([np.cos(angle), -np.sin(angle)])
    fwd[block] = 1.0 - 2.0 * (np.arange(block) % 2)
    out_pos = block + np.arange(block)[:, None]
    freq = np.arange(block)[None, :]
    angle = 2 * np.pi * ((freq * out_pos) % size) / size
    real = 2 * np.cos(angle)
    imag = -2 * np.sin(angle)
    real[:, 0] = 1.0
    imag[:, 0] = 1.0 - 2.0 * (np.arange(block) % 2)
    inv = np.concatenate([real, imag], 1) / size
    return fwd, fwd[:, ::-1], inv


def mm(a, b):
    return jnp.dot(a, b, preferred_element_type=jnp.float32)


def mm_wide(pair, values):
    high = values.astype(jnp.bfloat16)
    low = (values - high.astype(jnp.float32)).astype(jnp.bfloat16)
    return mm(pair[0], high) + mm(pair[0], low) + mm(pair[1], high)


def spectrum_parts(spec, block, row0):
    real, imag = spec[:block], spec[block:]
    return real, jnp.where(row0, 0.0, imag), jnp.where(row0, imag, real)


def spectrum_mul(parts, spec, block):
    real, imag, cross = parts
    sr, si = spec[:block], spec[block:]
    return real * sr - imag * si, cross * si + imag * sr


def fill(scratch, lead_rows, signal):
    scratch[:LEAD] = lead_rows.astype(jnp.float32)
    scratch[LEAD:] = signal.astype(jnp.float32)


def short_taps(scratch, filt, start, block):
    total = filt[0:1] * scratch[LEAD + start : LEAD + start + block]
    for lag in range(1, SHORT_LEN):
        first = LEAD + start - lag
        total = total + filt[lag : lag + 1] * scratch[first : first + block]
    return total


def local_kernel(
    k_ref, v_ref, lead_ref, filt_ref, taps_ref, res_ref, rate_ref, fwd_ref, rev_ref, inv_ref,
    y_ref, ends_ref, state_ref, tail_ref, ks, vs, gs,
):
    block = taps_ref.shape[0]
    pieces = k_ref.shape[0] // block
    modes = rate_ref.shape[0]
    fill(ks, lead_ref[1], k_ref[...])
    fill(vs, lead_ref[2], v_ref[...])
    for b in range(pieces):
        gated = short_taps(ks, filt_ref[1], b * block, block) * short_taps(
            vs, filt_ref[2], b * block, block
        )
        gs[b * block : (b + 1) * block] = gated.astype(jnp.bfloat16).astype(jnp.float32)
    rows = lax.broadcasted_iota(jnp.int32, (block, LANES), 0)
    back = (block - 1 - rows).astype(jnp.float32)

    def one_mode(n, h_rev):
        rate = rate_ref[pl.ds(n, 1), :]
        decay = jnp.exp(-rate * back)
        for b in range(pieces):
            ends_ref[n, b : b + 1, :] = jnp.sum(
                decay * gs[b * block : (b + 1) * block], axis=0, keepdims=True
            )
        return h_rev + (res_ref[pl.ds(n, 1), :] * jnp.sqrt(2.0 * rate)) * decay

    h_rev = lax.fori_loop(0, modes, one_mode, jnp.zeros((block, LANES), jnp.float32))

    step = jnp.exp(-rate_ref[...] * float(block))
    state = ends_ref[:, 0, :]
    for b in range(1, pieces):
        state = step * state + ends_ref[:, b, :]
    state_ref[...] = state

    row0 = rows == 0
    sign = (1 - 2 * (rows % 2)).astype(jnp.float32)
    sign = jnp.concatenate([sign, sign], 0)
    taps_spec = mm_wide(fwd_ref, taps_ref[...])
    near_spec = sign * (taps_spec + mm_wide(rev_ref, h_rev))
    far = spectrum_parts(taps_spec, block, row0)
    near = spectrum_parts(near_spec, block, row0)
    previous = None
    for b in range(pieces):
        signal = gs[b * block : (b + 1) * block].astype(jnp.bfloat16)
        spec = mm(fwd_ref[0], signal) + mm(fwd_ref[1], signal)
        real, imag = spectrum_mul(near, spec, block)
        if previous is not None:
            more_real, more_imag = spectrum_mul(far, previous, block)
            real, imag = real + more_real, imag + more_imag
        y_ref[b * block : (b + 1) * block] = mm_wide(inv_ref, jnp.concatenate([real, imag], 0))
        previous = spec
        if b == pieces - 1:
            tail_ref[...] = signal


def finish_kernel(
    y_ref, ends_ref, start_ref, tail_ref, q_ref, lead_ref, filt_ref, taps_ref, res_ref, rate_ref,
    fwd_ref, inv_ref, out_ref, qs, lift, states,
):
    block = taps_ref.shape[0]
    pieces = q_ref.shape[0] // block
    modes = rate_ref.shape[0]
    fill(qs, lead_ref[0], q_ref[...])
    rows = lax.broadcasted_iota(jnp.int32, (block, LANES), 0)
    ahead = (rows + 1).astype(jnp.float32)
    for n in range(modes):
        rate = rate_ref[n : n + 1, :]
        lift[n] = (res_ref[n : n + 1, :] * jnp.sqrt(2.0 * rate)) * jnp.exp(-rate * ahead)
    step = jnp.exp(-rate_ref[...] * float(block))
    state = start_ref[...]
    states[0] = state
    for b in range(1, pieces):
        state = step * state + ends_ref[:, b - 1, :]
        states[b] = state
    taps_spec = mm_wide(fwd_ref, taps_ref[...])
    far = spectrum_parts(taps_spec, block, rows == 0)
    tail = tail_ref[...]
    spec = mm(fwd_ref[0], tail) + mm(fwd_ref[1], tail)
    halo = mm_wide(inv_ref, jnp.concatenate(spectrum_mul(far, spec, block), 0))
    for b in range(pieces):
        span = slice(b * block, (b + 1) * block)
        total = y_ref[span]
        if b == 0:
            total = total + halo
        for n in range(modes):
            total = total + lift[n] * states[b, n : n + 1, :]
        q_short = short_taps(qs, filt_ref[0], b * block, block).astype(jnp.bfloat16)
        long_conv = total.astype(jnp.bfloat16)
        out_ref[span] = (q_short.astype(jnp.float32) * long_conv.astype(jnp.float32)).astype(
            jnp.bfloat16
        )


def cols(*lead):
    return pl.BlockSpec(lead + (LANES,), lambda i: (0,) * len(lead) + (i,))


def whole(shape):
    return pl.BlockSpec(shape, lambda i: (0,) * len(shape))


def local(q_in, k_in, v_in, short_filter, taps, residue, rate, out_weight):
    tokens, chans = q_in.shape
    block = taps.shape[0]
    modes = rate.shape[0]
    pieces = tokens // block
    fwd, rev, inv = [split_const(m) for m in dft_matrices(block)]
    grid = (chans // LANES,)
    f32, bf16 = jnp.float32, jnp.bfloat16
    lead = shifted(jnp.stack([q_in[-LEAD:], k_in[-LEAD:], v_in[-LEAD:]]), "ctx")
    filt_spec = cols(3, SHORT_LEN)
    params = pltpu.CompilerParams(vmem_limit_bytes=48 << 20)
    y_part, ends, state, tail = pl.pallas_call(
        local_kernel,
        grid=grid,
        in_specs=[
            cols(tokens), cols(tokens), cols(3, LEAD), filt_spec, cols(block), cols(modes),
            cols(modes), whole(fwd.shape), whole(rev.shape), whole(inv.shape),
        ],
        out_specs=[cols(tokens), cols(modes, pieces), cols(modes), cols(block)],
        out_shape=[
            jax.ShapeDtypeStruct((tokens, chans), f32),
            jax.ShapeDtypeStruct((modes, pieces, chans), f32),
            jax.ShapeDtypeStruct((modes, chans), f32),
            jax.ShapeDtypeStruct((block, chans), bf16),
        ],
        scratch_shapes=[
            pltpu.VMEM((LEAD + tokens, LANES), f32),
            pltpu.VMEM((LEAD + tokens, LANES), f32),
            pltpu.VMEM((tokens, LANES), f32),
        ],
        compiler_params=params,
        name="local_conv",
    )(k_in, v_in, lead, short_filter, taps, residue, rate, fwd, rev, inv)

    before = shifted(tail, "ctx")
    all_states = lax.all_gather(state, "ctx")
    gap = lax.axis_index("ctx") - 1 - jnp.arange(all_states.shape[0])
    spans = (jnp.maximum(gap, 0) * tokens).astype(f32)[:, None, None]
    carried = jnp.where((gap >= 0)[:, None, None], jnp.exp(-rate[None] * spans) * all_states, 0.0)
    start = jnp.sum(carried, axis=0)

    product = pl.pallas_call(
        finish_kernel,
        grid=grid,
        in_specs=[
            cols(tokens), cols(modes, pieces), cols(modes), cols(block), cols(tokens),
            cols(3, LEAD), filt_spec, cols(block), cols(modes), cols(modes),
            whole(fwd.shape), whole(inv.shape),
        ],
        out_specs=cols(tokens),
        out_shape=jax.ShapeDtypeStruct((tokens, chans), bf16),
        scratch_shapes=[
            pltpu.VMEM((LEAD + tokens, LANES), f32),
            pltpu.VMEM((modes, block, LANES), f32),
            pltpu.VMEM((pieces, modes, LANES), f32),
        ],
        compiler_params=params,
        name="finish_conv",
    )(y_part, ends, start, before, q_in, lead, short_filter, taps, residue, rate, fwd, inv)

    partial_sum = jnp.dot(
        product,
        lax.all_gather(out_weight, "ctx", axis=1, tiled=True),
        preferred_element_type=f32,
    )
    return lax.psum_scatter(partial_sum.astype(bf16), "mp", scatter_dimension=1, tiled=True)


def solution(mesh):
    in_specs = (
        P("ctx", "mp"),
        P("ctx", "mp"),
        P("ctx", "mp"),
        P(None, None, "mp"),
        P(None, "mp"),
        P(None, "mp"),
        P(None, "mp"),
        P("mp", "ctx"),
    )
    out_specs = P("ctx", "mp")
    return jax.shard_map(local, mesh=mesh, in_specs=in_specs, out_specs=out_specs, check_vma=False)
```

```python
import functools

import jax
import jax.numpy as jnp
import numpy as np
from jax import lax
from jax.experimental import pallas as pl
from jax.experimental.pallas import tpu as pltpu
from jax.sharding import PartitionSpec as P

SHORT_LEN = 7
LANES = 128
LEAD = 8


def shifted(array, axis):
    peers = lax.axis_size(axis)
    return lax.ppermute(array, axis, [(i, i + 1) for i in range(peers - 1)])


def split_const(matrix):
    high = matrix.astype(jnp.bfloat16)
    low = (matrix - high.astype(np.float64)).astype(jnp.bfloat16)
    return jnp.asarray(np.stack([high, low]))


@functools.lru_cache
def dft_matrices(block):
    size = 2 * block
    freq = np.arange(block)[:, None]
    pos = np.arange(block)[None, :]
    angle = 2 * np.pi * ((freq * pos) % size) / size
    fwd = np.concatenate([np.cos(angle), -np.sin(angle)])
    fwd[block] = 1.0 - 2.0 * (np.arange(block) % 2)
    out_pos = block + np.arange(block)[:, None]
    freq = np.arange(block)[None, :]
    angle = 2 * np.pi * ((freq * out_pos) % size) / size
    real = 2 * np.cos(angle)
    imag = -2 * np.sin(angle)
    real[:, 0] = 1.0
    imag[:, 0] = 1.0 - 2.0 * (np.arange(block) % 2)
    inv = np.concatenate([real, imag], 1) / size
    return fwd, fwd[:, ::-1], inv


def mm(a, b):
    return jnp.dot(a, b, preferred_element_type=jnp.float32)


def mm_wide(pair, values):
    high = values.astype(jnp.bfloat16)
    low = (values - high.astype(jnp.float32)).astype(jnp.bfloat16)
    return mm(pair[0], high) + mm(pair[0], low) + mm(pair[1], high)


def spectrum_parts(spec, block, row0):
    real, imag = spec[:block], spec[block:]
    return real, jnp.where(row0, 0.0, imag), jnp.where(row0, imag, real)


def spectrum_mul(parts, spec, block):
    real, imag, cross = parts
    sr, si = spec[:block], spec[block:]
    return real * sr - imag * si, cross * si + imag * sr


def fill(scratch, lead_rows, signal):
    scratch[:LEAD] = lead_rows.astype(jnp.float32)
    scratch[LEAD:] = signal.astype(jnp.float32)


def short_taps(scratch, filt, start, block):
    total = filt[0:1] * scratch[LEAD + start : LEAD + start + block]
    for lag in range(1, SHORT_LEN):
        first = LEAD + start - lag
        total = total + filt[lag : lag + 1] * scratch[first : first + block]
    return total


def local_kernel(
    k_ref, v_ref, lead_ref, filt_ref, taps_ref, res_ref, rate_ref, fwd_ref, rev_ref, inv_ref,
    y_ref, ends_ref, state_ref, tail_ref, ks, vs, gs,
):
    block = taps_ref.shape[0]
    pieces = k_ref.shape[0] // block
    modes = rate_ref.shape[0]
    fill(ks, lead_ref[1], k_ref[...])
    fill(vs, lead_ref[2], v_ref[...])
    for b in range(pieces):
        gated = short_taps(ks, filt_ref[1], b * block, block) * short_taps(
            vs, filt_ref[2], b * block, block
        )
        gs[b * block : (b + 1) * block] = gated.astype(jnp.bfloat16).astype(jnp.float32)
    rows = lax.broadcasted_iota(jnp.int32, (block, LANES), 0)
    back = (block - 1 - rows).astype(jnp.float32)

    def one_mode(n, h_rev):
        rate = rate_ref[pl.ds(n, 1), :]
        decay = jnp.exp(-rate * back)
        for b in range(pieces):
            ends_ref[n, b : b + 1, :] = jnp.sum(
                decay * gs[b * block : (b + 1) * block], axis=0, keepdims=True
            )
        return h_rev + (res_ref[pl.ds(n, 1), :] * jnp.sqrt(2.0 * rate)) * decay

    h_rev = lax.fori_loop(0, modes, one_mode, jnp.zeros((block, LANES), jnp.float32))

    step = jnp.exp(-rate_ref[...] * float(block))
    state = ends_ref[:, 0, :]
    for b in range(1, pieces):
        state = step * state + ends_ref[:, b, :]
    state_ref[...] = state

    row0 = rows == 0
    sign = (1 - 2 * (rows % 2)).astype(jnp.float32)
    sign = jnp.concatenate([sign, sign], 0)
    taps_spec = mm_wide(fwd_ref, taps_ref[...])
    near_spec = sign * (taps_spec + mm_wide(rev_ref, h_rev))
    far = spectrum_parts(taps_spec, block, row0)
    near = spectrum_parts(near_spec, block, row0)
    previous = None
    for b in range(pieces):
        signal = gs[b * block : (b + 1) * block].astype(jnp.bfloat16)
        spec = mm(fwd_ref[0], signal) + mm(fwd_ref[1], signal)
        real, imag = spectrum_mul(near, spec, block)
        if previous is not None:
            more_real, more_imag = spectrum_mul(far, previous, block)
            real, imag = real + more_real, imag + more_imag
        y_ref[b * block : (b + 1) * block] = mm_wide(inv_ref, jnp.concatenate([real, imag], 0))
        previous = spec
        if b == pieces - 1:
            tail_ref[...] = signal


def finish_kernel(
    y_ref, ends_ref, start_ref, tail_ref, q_ref, lead_ref, filt_ref, taps_ref, res_ref, rate_ref,
    fwd_ref, inv_ref, out_ref, qs, lift, states,
):
    block = taps_ref.shape[0]
    pieces = q_ref.shape[0] // block
    modes = rate_ref.shape[0]
    fill(qs, lead_ref[0], q_ref[...])
    rows = lax.broadcasted_iota(jnp.int32, (block, LANES), 0)
    ahead = (rows + 1).astype(jnp.float32)
    for n in range(modes):
        rate = rate_ref[n : n + 1, :]
        lift[n] = (res_ref[n : n + 1, :] * jnp.sqrt(2.0 * rate)) * jnp.exp(-rate * ahead)
    step = jnp.exp(-rate_ref[...] * float(block))
    state = start_ref[...]
    states[0] = state
    for b in range(1, pieces):
        state = step * state + ends_ref[:, b - 1, :]
        states[b] = state
    taps_spec = mm_wide(fwd_ref, taps_ref[...])
    far = spectrum_parts(taps_spec, block, rows == 0)
    tail = tail_ref[...]
    spec = mm(fwd_ref[0], tail) + mm(fwd_ref[1], tail)
    halo = mm_wide(inv_ref, jnp.concatenate(spectrum_mul(far, spec, block), 0))
    for b in range(pieces):
        span = slice(b * block, (b + 1) * block)
        total = y_ref[span]
        if b == 0:
            total = total + halo
        for n in range(modes):
            total = total + lift[n] * states[b, n : n + 1, :]
        q_short = short_taps(qs, filt_ref[0], b * block, block).astype(jnp.bfloat16)
        long_conv = total.astype(jnp.bfloat16)
        out_ref[span] = (q_short.astype(jnp.float32) * long_conv.astype(jnp.float32)).astype(
            jnp.bfloat16
        )

MESH = pl.DeviceIdType.MESH


def exchange_kernel(peers, state_ref, tail_ref, all_ref, before_ref, send, recv, tail_sems):
    me = lax.axis_index("ctx")
    barrier = pltpu.get_barrier_semaphore()
    for hop in range(1, peers):
        pl.semaphore_signal(
            barrier, inc=1, device_id={"ctx": lax.rem(me + hop, peers)}, device_id_type=MESH
        )
    pl.semaphore_wait(barrier, peers - 1)

    def tail_copy(peer):
        return pltpu.make_async_remote_copy(
            src_ref=tail_ref, dst_ref=before_ref, send_sem=tail_sems.at[0],
            recv_sem=tail_sems.at[1], device_id={"ctx": peer}, device_id_type=MESH,
        )

    def state_copy(peer, slot, hop):
        return pltpu.make_async_remote_copy(
            src_ref=state_ref, dst_ref=all_ref.at[slot], send_sem=send.at[hop],
            recv_sem=recv.at[slot], device_id={"ctx": peer}, device_id_type=MESH,
        )

    @pl.when(me < peers - 1)
    def _():
        tail_copy(me + 1).start()

    for hop in range(1, peers):
        state_copy(lax.rem(me + hop, peers), me, hop).start()
    all_ref[me] = state_ref[...]

    @pl.when(me == 0)
    def _():
        before_ref[...] = jnp.zeros_like(before_ref)

    for hop in range(1, peers):
        source = lax.rem(me + hop, peers)
        state_copy(source, source, hop).wait_recv()
        state_copy(source, me, hop).wait_send()

    @pl.when(me > 0)
    def _():
        tail_copy(me).wait_recv()

    @pl.when(me < peers - 1)
    def _():
        tail_copy(me + 1).wait_send()


def exchange(state, tail):
    peers = lax.axis_size("ctx")
    vmem = pl.BlockSpec(memory_space=pltpu.VMEM)
    return pl.pallas_call(
        functools.partial(exchange_kernel, peers),
        in_specs=[vmem] * 2,
        out_specs=[vmem] * 2,
        out_shape=[
            jax.ShapeDtypeStruct((peers,) + state.shape, state.dtype),
            jax.ShapeDtypeStruct(tail.shape, tail.dtype),
        ],
        scratch_shapes=[
            pltpu.SemaphoreType.DMA((peers,)),
            pltpu.SemaphoreType.DMA((peers,)),
            pltpu.SemaphoreType.DMA((2,)),
        ],
        compiler_params=pltpu.CompilerParams(collective_id=0, has_side_effects=True),
        name="state_exchange",
    )(state, tail)


def project_kernel(
    prod_ref, w_ref, out_ref, near_out, near_in, far_out, far_in, mine_out, mine_in, hold, total,
    sems,
):
    me = lax.axis_index("mp")
    high, low = me // 2, lax.rem(me, 2)
    pair = high * 2 + (1 - low)
    across = (1 - high) * 2 + low
    chunks, rows, width = near_out.shape
    step = 256

    barrier = pltpu.get_barrier_semaphore()
    for peer in (pair, across):
        pl.semaphore_signal(barrier, inc=1, device_id={"mp": peer}, device_id_type=MESH)
    pl.semaphore_wait(barrier, 2)

    def copy(kind, t, source, target, peer):
        return pltpu.make_async_remote_copy(
            src_ref=source.at[t], dst_ref=target.at[t], send_sem=sems.at[2 * kind, t],
            recv_sem=sems.at[2 * kind + 1, t], device_id={"mp": peer}, device_id_type=MESH,
        )

    def near_copy(t):
        return copy(0, t, near_out, near_in, pair)

    def far_copy(t):
        return copy(1, t, far_out, far_in, across)

    def mine_copy(t):
        return copy(2, t, mine_out, mine_in, pair)

    def partial(t, owner, put):
        left = prod_ref[pl.ds(pl.multiple_of(t * rows, rows), rows), :]
        for col in range(0, width, step):
            first = pl.multiple_of(owner * width + col, step)
            put(col, mm(left, w_ref[:, pl.ds(first, step)]))

    def send_near(t):
        def put(col, value):
            near_out[t, :, col : col + step] = value.astype(jnp.bfloat16)

        partial(t, (1 - high) * 2 + (1 - low), put)
        near_copy(t).start()

        def keep(col, value):
            hold[t, :, col : col + step] = value

        partial(t, across, keep)

    def send_far(t):
        near_copy(t).wait_recv()
        far_out[t] = (hold[t] + near_in[t].astype(jnp.float32)).astype(jnp.bfloat16)
        far_copy(t).start()

    def first_pass(t, carry):
        send_near(t)

        @pl.when(t > 0)
        def _():
            send_far(t - 1)

        return carry

    lax.fori_loop(0, chunks, first_pass, 0)
    send_far(chunks - 1)

    def second_pass(t, carry):
        def put(col, value):
            mine_out[t, :, col : col + step] = value.astype(jnp.bfloat16)

        partial(t, pair, put)
        mine_copy(t).start()

        def keep(col, value):
            total[t, :, col : col + step] = value

        partial(t, me, keep)
        return carry

    lax.fori_loop(0, chunks, second_pass, 0)

    def finish(t, carry):
        mine_copy(t).wait_recv()
        far_copy(t).wait_recv()
        summed = total[t] + mine_in[t].astype(jnp.float32) + far_in[t].astype(jnp.float32)
        out_ref[pl.ds(pl.multiple_of(t * rows, rows), rows), :] = summed.astype(jnp.bfloat16)
        near_copy(t).wait_send()
        far_copy(t).wait_send()
        mine_copy(t).wait_send()
        return carry

    lax.fori_loop(0, chunks, finish, 0)


def project(product, weight):
    tokens = product.shape[0]
    width = weight.shape[1] // lax.axis_size("mp")
    chunks = 8
    box = (chunks, tokens // chunks, width)
    vmem = pl.BlockSpec(memory_space=pltpu.VMEM)
    return pl.pallas_call(
        project_kernel,
        in_specs=[vmem] * 2,
        out_specs=vmem,
        out_shape=jax.ShapeDtypeStruct((tokens, width), jnp.bfloat16),
        scratch_shapes=[pltpu.VMEM(box, jnp.bfloat16)] * 6
        + [pltpu.VMEM(box, jnp.float32)] * 2
        + [pltpu.SemaphoreType.DMA((6, chunks))],
        compiler_params=pltpu.CompilerParams(
            collective_id=1, has_side_effects=True, vmem_limit_bytes=48 << 20
        ),
        name="project",
    )(product, weight)


def cols(*lead):
    return pl.BlockSpec(lead + (LANES,), lambda i: (0,) * len(lead) + (i,))


def whole(shape):
    return pl.BlockSpec(shape, lambda i: (0,) * len(shape))


def local(q_in, k_in, v_in, short_filter, taps, residue, rate, out_weight):
    tokens, chans = q_in.shape
    block = taps.shape[0]
    modes = rate.shape[0]
    pieces = tokens // block
    fwd, rev, inv = [split_const(m) for m in dft_matrices(block)]
    grid = (chans // LANES,)
    f32, bf16 = jnp.float32, jnp.bfloat16
    lead = shifted(jnp.stack([q_in[-LEAD:], k_in[-LEAD:], v_in[-LEAD:]]), "ctx")
    filt_spec = cols(3, SHORT_LEN)
    params = pltpu.CompilerParams(vmem_limit_bytes=48 << 20)
    y_part, ends, state, tail = pl.pallas_call(
        local_kernel,
        grid=grid,
        in_specs=[
            cols(tokens), cols(tokens), cols(3, LEAD), filt_spec, cols(block), cols(modes),
            cols(modes), whole(fwd.shape), whole(rev.shape), whole(inv.shape),
        ],
        out_specs=[cols(tokens), cols(modes, pieces), cols(modes), cols(block)],
        out_shape=[
            jax.ShapeDtypeStruct((tokens, chans), f32),
            jax.ShapeDtypeStruct((modes, pieces, chans), f32),
            jax.ShapeDtypeStruct((modes, chans), f32),
            jax.ShapeDtypeStruct((block, chans), bf16),
        ],
        scratch_shapes=[
            pltpu.VMEM((LEAD + tokens, LANES), f32),
            pltpu.VMEM((LEAD + tokens, LANES), f32),
            pltpu.VMEM((tokens, LANES), f32),
        ],
        compiler_params=params,
        name="local_conv",
    )(k_in, v_in, lead, short_filter, taps, residue, rate, fwd, rev, inv)

    all_states, before = exchange(state, tail)
    gap = lax.axis_index("ctx") - 1 - jnp.arange(all_states.shape[0])
    spans = (jnp.maximum(gap, 0) * tokens).astype(f32)[:, None, None]
    carried = jnp.where((gap >= 0)[:, None, None], jnp.exp(-rate[None] * spans) * all_states, 0.0)
    start = jnp.sum(carried, axis=0)

    product = pl.pallas_call(
        finish_kernel,
        grid=grid,
        in_specs=[
            cols(tokens), cols(modes, pieces), cols(modes), cols(block), cols(tokens),
            cols(3, LEAD), filt_spec, cols(block), cols(modes), cols(modes),
            whole(fwd.shape), whole(inv.shape),
        ],
        out_specs=cols(tokens),
        out_shape=jax.ShapeDtypeStruct((tokens, chans), bf16),
        scratch_shapes=[
            pltpu.VMEM((LEAD + tokens, LANES), f32),
            pltpu.VMEM((modes, block, LANES), f32),
            pltpu.VMEM((pieces, modes, LANES), f32),
        ],
        compiler_params=params,
        name="finish_conv",
    )(y_part, ends, start, before, q_in, lead, short_filter, taps, residue, rate, fwd, inv)

    return project(product, lax.all_gather(out_weight, "ctx", axis=1, tiled=True))


def solution(mesh):
    in_specs = (
        P("ctx", "mp"),
        P("ctx", "mp"),
        P("ctx", "mp"),
        P(None, None, "mp"),
        P(None, "mp"),
        P(None, "mp"),
        P(None, "mp"),
        P("mp", "ctx"),
    )
    out_specs = P("ctx", "mp")
    return jax.shard_map(local, mesh=mesh, in_specs=in_specs, out_specs=out_specs, check_vma=False)
```

```python
import functools

import jax
import jax.numpy as jnp
import numpy as np
from jax import lax
from jax.experimental import pallas as pl
from jax.experimental.pallas import tpu as pltpu
from jax.sharding import PartitionSpec as P

SHORT_LEN = 7
LANES = 128
LEAD = 8


def shifted(array, axis):
    peers = lax.axis_size(axis)
    return lax.ppermute(array, axis, [(i, i + 1) for i in range(peers - 1)])


def split_const(matrix):
    high = matrix.astype(jnp.bfloat16)
    low = (matrix - high.astype(np.float64)).astype(jnp.bfloat16)
    return jnp.asarray(np.stack([high, low]))


@functools.lru_cache
def dft_matrices(block):
    size = 2 * block
    freq = np.arange(block)[:, None]
    pos = np.arange(block)[None, :]
    angle = 2 * np.pi * ((freq * pos) % size) / size
    fwd = np.concatenate([np.cos(angle), -np.sin(angle)])
    fwd[block] = 1.0 - 2.0 * (np.arange(block) % 2)
    out_pos = block + np.arange(block)[:, None]
    freq = np.arange(block)[None, :]
    angle = 2 * np.pi * ((freq * out_pos) % size) / size
    real = 2 * np.cos(angle)
    imag = -2 * np.sin(angle)
    real[:, 0] = 1.0
    imag[:, 0] = 1.0 - 2.0 * (np.arange(block) % 2)
    inv = np.concatenate([real, imag], 1) / size
    return fwd, fwd[:, ::-1], inv


def mm(a, b):
    return jnp.dot(a, b, preferred_element_type=jnp.float32)


def mm_wide(pair, values):
    high = values.astype(jnp.bfloat16)
    low = (values - high.astype(jnp.float32)).astype(jnp.bfloat16)
    return mm(pair[0], high) + mm(pair[0], low) + mm(pair[1], high)


def spectrum_parts(spec, block, row0):
    real, imag = spec[:block], spec[block:]
    return real, jnp.where(row0, 0.0, imag), jnp.where(row0, imag, real)


def spectrum_mul(parts, spec, block):
    real, imag, cross = parts
    sr, si = spec[:block], spec[block:]
    return real * sr - imag * si, cross * si + imag * sr


def fill(scratch, lead_rows, signal):
    scratch[:LEAD] = lead_rows.astype(jnp.float32)
    scratch[LEAD:] = signal.astype(jnp.float32)


def short_taps(scratch, filt, start, block):
    total = filt[0:1] * scratch[LEAD + start : LEAD + start + block]
    for lag in range(1, SHORT_LEN):
        first = LEAD + start - lag
        total = total + filt[lag : lag + 1] * scratch[first : first + block]
    return total


def local_kernel(
    k_ref, v_ref, lead_ref, filt_ref, taps_ref, res_ref, rate_ref, fwd_ref, rev_ref, inv_ref,
    y_ref, ends_ref, state_ref, tail_ref, ks, vs, gs,
):
    block = taps_ref.shape[0]
    pieces = k_ref.shape[0] // block
    modes = rate_ref.shape[0]
    fill(ks, lead_ref[1], k_ref[...])
    fill(vs, lead_ref[2], v_ref[...])
    for b in range(pieces):
        gated = short_taps(ks, filt_ref[1], b * block, block) * short_taps(
            vs, filt_ref[2], b * block, block
        )
        gs[b * block : (b + 1) * block] = gated.astype(jnp.bfloat16).astype(jnp.float32)
    rows = lax.broadcasted_iota(jnp.int32, (block, LANES), 0)
    back = (block - 1 - rows).astype(jnp.float32)

    def one_mode(n, h_rev):
        rate = rate_ref[pl.ds(n, 1), :]
        decay = jnp.exp(-rate * back)
        for b in range(pieces):
            ends_ref[n, b : b + 1, :] = jnp.sum(
                decay * gs[b * block : (b + 1) * block], axis=0, keepdims=True
            )
        return h_rev + (res_ref[pl.ds(n, 1), :] * jnp.sqrt(2.0 * rate)) * decay

    h_rev = lax.fori_loop(0, modes, one_mode, jnp.zeros((block, LANES), jnp.float32))

    step = jnp.exp(-rate_ref[...] * float(block))
    state = ends_ref[:, 0, :]
    for b in range(1, pieces):
        state = step * state + ends_ref[:, b, :]
    state_ref[...] = state

    row0 = rows == 0
    sign = (1 - 2 * (rows % 2)).astype(jnp.float32)
    sign = jnp.concatenate([sign, sign], 0)
    taps_spec = mm_wide(fwd_ref, taps_ref[...])
    near_spec = sign * (taps_spec + mm_wide(rev_ref, h_rev))
    far = spectrum_parts(taps_spec, block, row0)
    near = spectrum_parts(near_spec, block, row0)
    previous = None
    for b in range(pieces):
        signal = gs[b * block : (b + 1) * block].astype(jnp.bfloat16)
        spec = mm(fwd_ref[0], signal) + mm(fwd_ref[1], signal)
        real, imag = spectrum_mul(near, spec, block)
        if previous is not None:
            more_real, more_imag = spectrum_mul(far, previous, block)
            real, imag = real + more_real, imag + more_imag
        y_ref[b * block : (b + 1) * block] = mm_wide(inv_ref, jnp.concatenate([real, imag], 0))
        previous = spec
        if b == pieces - 1:
            tail_ref[...] = signal


def finish_kernel(
    y_ref, ends_ref, start_ref, tail_ref, q_ref, lead_ref, filt_ref, taps_ref, res_ref, rate_ref,
    fwd_ref, inv_ref, out_ref, qs, lift, states,
):
    block = taps_ref.shape[0]
    pieces = q_ref.shape[0] // block
    modes = rate_ref.shape[0]
    fill(qs, lead_ref[0], q_ref[...])
    rows = lax.broadcasted_iota(jnp.int32, (block, LANES), 0)
    ahead = (rows + 1).astype(jnp.float32)
    for n in range(modes):
        rate = rate_ref[n : n + 1, :]
        lift[n] = (res_ref[n : n + 1, :] * jnp.sqrt(2.0 * rate)) * jnp.exp(-rate * ahead)
    step = jnp.exp(-rate_ref[...] * float(block))
    state = start_ref[...]
    states[0] = state
    for b in range(1, pieces):
        state = step * state + ends_ref[:, b - 1, :]
        states[b] = state
    taps_spec = mm_wide(fwd_ref, taps_ref[...])
    far = spectrum_parts(taps_spec, block, rows == 0)
    tail = tail_ref[...]
    spec = mm(fwd_ref[0], tail) + mm(fwd_ref[1], tail)
    halo = mm_wide(inv_ref, jnp.concatenate(spectrum_mul(far, spec, block), 0))
    for b in range(pieces):
        span = slice(b * block, (b + 1) * block)
        total = y_ref[span]
        if b == 0:
            total = total + halo
        for n in range(modes):
            total = total + lift[n] * states[b, n : n + 1, :]
        q_short = short_taps(qs, filt_ref[0], b * block, block).astype(jnp.bfloat16)
        long_conv = total.astype(jnp.bfloat16)
        out_ref[span] = (q_short.astype(jnp.float32) * long_conv.astype(jnp.float32)).astype(
            jnp.bfloat16
        )

MESH = pl.DeviceIdType.MESH


def exchange_kernel(peers, state_ref, tail_ref, all_ref, before_ref, send, recv, tail_sems):
    me = lax.axis_index("ctx")
    barrier = pltpu.get_barrier_semaphore()
    for hop in range(1, peers):
        pl.semaphore_signal(
            barrier, inc=1, device_id={"ctx": lax.rem(me + hop, peers)}, device_id_type=MESH
        )
    pl.semaphore_wait(barrier, peers - 1)

    def tail_copy(peer):
        return pltpu.make_async_remote_copy(
            src_ref=tail_ref, dst_ref=before_ref, send_sem=tail_sems.at[0],
            recv_sem=tail_sems.at[1], device_id={"ctx": peer}, device_id_type=MESH,
        )

    def state_copy(peer, slot, hop):
        return pltpu.make_async_remote_copy(
            src_ref=state_ref, dst_ref=all_ref.at[slot], send_sem=send.at[hop],
            recv_sem=recv.at[slot], device_id={"ctx": peer}, device_id_type=MESH,
        )

    @pl.when(me < peers - 1)
    def _():
        tail_copy(me + 1).start()

    for hop in range(1, peers):
        state_copy(lax.rem(me + hop, peers), me, hop).start()
    all_ref[me] = state_ref[...]

    @pl.when(me == 0)
    def _():
        before_ref[...] = jnp.zeros_like(before_ref)

    for hop in range(1, peers):
        source = lax.rem(me + hop, peers)
        state_copy(source, source, hop).wait_recv()
        state_copy(source, me, hop).wait_send()

    @pl.when(me > 0)
    def _():
        tail_copy(me).wait_recv()

    @pl.when(me < peers - 1)
    def _():
        tail_copy(me + 1).wait_send()


def exchange(state, tail):
    peers = lax.axis_size("ctx")
    vmem = pl.BlockSpec(memory_space=pltpu.VMEM)
    return pl.pallas_call(
        functools.partial(exchange_kernel, peers),
        in_specs=[vmem] * 2,
        out_specs=[vmem] * 2,
        out_shape=[
            jax.ShapeDtypeStruct((peers,) + state.shape, state.dtype),
            jax.ShapeDtypeStruct(tail.shape, tail.dtype),
        ],
        scratch_shapes=[
            pltpu.SemaphoreType.DMA((peers,)),
            pltpu.SemaphoreType.DMA((peers,)),
            pltpu.SemaphoreType.DMA((2,)),
        ],
        compiler_params=pltpu.CompilerParams(collective_id=0, has_side_effects=True),
        name="state_exchange",
    )(state, tail)


def project_kernel(
    prod_ref, w_ref, out_ref, near_out, near_in, far_out, far_in, mine_out, mine_in, hold, total,
    sems,
):
    me = lax.axis_index("mp")
    high, low = me // 2, lax.rem(me, 2)
    pair = high * 2 + (1 - low)
    across = (1 - high) * 2 + low
    chunks, rows, width = near_out.shape
    step = 256

    barrier = pltpu.get_barrier_semaphore()
    for peer in (pair, across):
        pl.semaphore_signal(barrier, inc=1, device_id={"mp": peer}, device_id_type=MESH)
    pl.semaphore_wait(barrier, 2)

    def copy(kind, t, source, target, peer):
        return pltpu.make_async_remote_copy(
            src_ref=source.at[t], dst_ref=target.at[t], send_sem=sems.at[2 * kind, t],
            recv_sem=sems.at[2 * kind + 1, t], device_id={"mp": peer}, device_id_type=MESH,
        )

    def near_copy(t):
        return copy(0, t, near_out, near_in, pair)

    def far_copy(t):
        return copy(1, t, far_out, far_in, across)

    def mine_copy(t):
        return copy(2, t, mine_out, mine_in, pair)

    def partial(t, owner, put):
        left = prod_ref[pl.ds(pl.multiple_of(t * rows, rows), rows), :]
        for col in range(0, width, step):
            first = pl.multiple_of(owner * width + col, step)
            put(col, mm(left, w_ref[:, pl.ds(first, step)]))

    def send_near(t):
        def put(col, value):
            near_out[t, :, col : col + step] = value.astype(jnp.bfloat16)

        partial(t, (1 - high) * 2 + (1 - low), put)
        near_copy(t).start()

        def keep(col, value):
            hold[t, :, col : col + step] = value

        partial(t, across, keep)

    def send_far(t):
        near_copy(t).wait_recv()
        far_out[t] = (hold[t] + near_in[t].astype(jnp.float32)).astype(jnp.bfloat16)
        far_copy(t).start()

    def first_pass(t, carry):
        send_near(t)

        @pl.when(t > 0)
        def _():
            send_far(t - 1)

        return carry

    lax.fori_loop(0, chunks, first_pass, 0)
    send_far(chunks - 1)

    def second_pass(t, carry):
        def put(col, value):
            mine_out[t, :, col : col + step] = value.astype(jnp.bfloat16)

        partial(t, pair, put)
        mine_copy(t).start()

        def keep(col, value):
            total[t, :, col : col + step] = value

        partial(t, me, keep)
        return carry

    lax.fori_loop(0, chunks, second_pass, 0)

    def finish(t, carry):
        mine_copy(t).wait_recv()
        far_copy(t).wait_recv()
        summed = total[t] + mine_in[t].astype(jnp.float32) + far_in[t].astype(jnp.float32)
        out_ref[pl.ds(pl.multiple_of(t * rows, rows), rows), :] = summed.astype(jnp.bfloat16)
        near_copy(t).wait_send()
        far_copy(t).wait_send()
        mine_copy(t).wait_send()
        return carry

    lax.fori_loop(0, chunks, finish, 0)


def project(product, weight):
    tokens = product.shape[0]
    width = weight.shape[1] // lax.axis_size("mp")
    chunks = 8
    box = (chunks, tokens // chunks, width)
    vmem = pl.BlockSpec(memory_space=pltpu.VMEM)
    return pl.pallas_call(
        project_kernel,
        in_specs=[vmem] * 2,
        out_specs=vmem,
        out_shape=jax.ShapeDtypeStruct((tokens, width), jnp.bfloat16),
        scratch_shapes=[pltpu.VMEM(box, jnp.bfloat16)] * 6
        + [pltpu.VMEM(box, jnp.float32)] * 2
        + [pltpu.SemaphoreType.DMA((6, chunks))],
        compiler_params=pltpu.CompilerParams(
            collective_id=1, has_side_effects=True, vmem_limit_bytes=48 << 20
        ),
        name="project",
    )(product, weight)


def ring_place(chip, count):
    odd = chip % 2
    return (chip // 2) * (1 - odd) + (count - 1 - chip // 2) * odd


def ring_chip(place, count):
    back = place // (count // 2)
    return 2 * place * (1 - back) + (2 * (count - 1 - place) + 1) * back


def ring_project_kernel(
    peers, prod_ref, w_ref, own_ref, out_ref, near_out, near_in, far_out, far_in, mine_out,
    mine_in, hold, total, ring, pair_out, pair_in, cross_out, cross_in, kept, sems, ring_sems,
    unit_sems,
):
    me = lax.axis_index("mp")
    high, low = me // 2, lax.rem(me, 2)
    pair = high * 2 + (1 - low)
    across = (1 - high) * 2 + low
    place = ring_place(lax.axis_index("ctx"), peers)
    chunks, rows, width = near_out.shape
    step = own_ref.shape[1]
    row_step = 256

    def neighbour(offset):
        return lax.rem(place + offset + peers, peers)

    ahead, behind = ring_chip(neighbour(1), peers), ring_chip(neighbour(-1), peers)
    barrier = pltpu.get_barrier_semaphore()
    for peer in (pair, across):
        pl.semaphore_signal(barrier, inc=1, device_id={"mp": peer}, device_id_type=MESH)
    for peer in (ahead, behind):
        pl.semaphore_signal(barrier, inc=1, device_id={"ctx": peer}, device_id_type=MESH)
    pl.semaphore_wait(barrier, 4)

    def ring_copy(way, hop, first):
        owner = ring_chip(neighbour(-hop if way == 0 else hop), peers)
        return pltpu.make_async_remote_copy(
            src_ref=own_ref if first else ring.at[owner], dst_ref=ring.at[owner],
            send_sem=ring_sems.at[2 * way, hop], recv_sem=ring_sems.at[2 * way + 1, hop],
            device_id={"ctx": behind if way else ahead}, device_id_type=MESH,
        )

    hops = (peers // 2, peers - 1 - peers // 2)
    for way in (0, 1):
        ring_copy(way, 0, True).start()

    def copy(kind, t, source, target, peer):
        return pltpu.make_async_remote_copy(
            src_ref=source.at[t], dst_ref=target.at[t], send_sem=sems.at[2 * kind, t],
            recv_sem=sems.at[2 * kind + 1, t], device_id={"mp": peer}, device_id_type=MESH,
        )

    def near_copy(t):
        return copy(0, t, near_out, near_in, pair)

    def far_copy(t):
        return copy(1, t, far_out, far_in, across)

    def mine_copy(t):
        return copy(2, t, mine_out, mine_in, pair)

    def partial(t, owner, put):
        left = prod_ref[pl.ds(pl.multiple_of(t * rows, rows), rows), :]
        for col in range(0, width, step):
            first = pl.multiple_of(owner * width + col, step)
            put(col, mm(left, w_ref[:, pl.ds(first, step)]))

    def send_far(t):
        near_copy(t).wait_recv()
        far_out[t] = (hold[t] + near_in[t].astype(jnp.float32)).astype(jnp.bfloat16)
        far_copy(t).start()

    def first_pass(t, carry):
        def put(col, value):
            near_out[t, :, col : col + step] = value.astype(jnp.bfloat16)

        partial(t, (1 - high) * 2 + (1 - low), put)
        near_copy(t).start()

        def keep(col, value):
            hold[t, :, col : col + step] = value

        partial(t, across, keep)

        @pl.when(t > 0)
        def _():
            send_far(t - 1)

        return carry

    lax.fori_loop(0, chunks, first_pass, 0)
    send_far(chunks - 1)

    def second_pass(t, carry):
        def put(col, value):
            mine_out[t, :, col : col + step] = value.astype(jnp.bfloat16)

        partial(t, pair, put)
        mine_copy(t).start()

        def keep(col, value):
            total[t, :, col : col + step] = value

        partial(t, me, keep)
        return carry

    lax.fori_loop(0, chunks, second_pass, 0)

    def pair_copy(slot):
        return pltpu.make_async_remote_copy(
            src_ref=pair_out.at[slot], dst_ref=pair_in.at[slot], send_sem=unit_sems.at[0, slot],
            recv_sem=unit_sems.at[1, slot], device_id={"mp": pair}, device_id_type=MESH,
        )

    def cross_copy(slot):
        return pltpu.make_async_remote_copy(
            src_ref=cross_out.at[slot], dst_ref=cross_in.at[slot],
            send_sem=unit_sems.at[2, slot], recv_sem=unit_sems.at[3, slot],
            device_id={"mp": across}, device_id_type=MESH,
        )

    def unit(chip, first):
        owner, sub = chip // 2, lax.rem(chip, 2)
        gap = owner // 2 - high
        same = 1 - gap * gap
        slot = same * 2 + sub
        mine = lax.rem(owner, 2) == low

        def products(put):
            def body(r, carry):
                at = pl.ds(pl.multiple_of(r * row_step, row_step), row_step)
                right = own_ref[...] if first else ring[chip]
                put(at, mm(prod_ref[at, :], right))
                return carry

            lax.fori_loop(0, prod_ref.shape[0] // row_step, body, 0)

        @pl.when(jnp.logical_not(mine))
        def _():
            def put(at, value):
                pair_out[slot, at, :] = value.astype(jnp.bfloat16)

            products(put)
            pair_copy(slot).start()

        @pl.when(mine)
        def _():
            def put(at, value):
                kept[slot, at, :] = value

            products(put)

            @pl.when(same == 0)
            def _():
                pair_copy(slot).wait_recv()
                cross_out[sub] = (kept[slot] + pair_in[slot].astype(jnp.float32)).astype(
                    jnp.bfloat16
                )
                cross_copy(sub).start()

    unit(ring_chip(place, peers), True)

    def arrived(way, hop):
        return ring_chip(neighbour(-hop - 1 if way == 0 else hop + 1), peers)

    for hop in range(hops[0]):
        ways = [way for way in (0, 1) if hop < hops[way]]
        for way in ways:
            pltpu.make_async_remote_copy(
                src_ref=own_ref, dst_ref=ring.at[arrived(way, hop)],
                send_sem=ring_sems.at[2 * way, hop], recv_sem=ring_sems.at[2 * way + 1, hop],
                device_id={"ctx": behind if way else ahead}, device_id_type=MESH,
            ).wait_recv()
            if hop + 1 < hops[way]:
                ring_copy(way, hop + 1, False).start()
        for way in ways:
            unit(arrived(way, hop), False)

    def finish(t, carry):
        mine_copy(t).wait_recv()
        far_copy(t).wait_recv()
        summed = total[t] + mine_in[t].astype(jnp.float32) + far_in[t].astype(jnp.float32)
        at = pl.ds(pl.multiple_of(t * rows, rows), rows)
        for part in range(width // step):
            out_ref[at, 2 * part * step : (2 * part + 1) * step] = summed[
                :, part * step : (part + 1) * step
            ].astype(jnp.bfloat16)
        near_copy(t).wait_send()
        far_copy(t).wait_send()
        mine_copy(t).wait_send()
        return carry

    lax.fori_loop(0, chunks, finish, 0)
    for sub in range(2):
        pair_copy(2 + sub).wait_recv()
        cross_copy(sub).wait_recv()
        summed = kept[2 + sub] + pair_in[2 + sub].astype(jnp.float32)
        out_ref[:, (2 * sub + 1) * step : (2 * sub + 2) * step] = (
            summed + cross_in[sub].astype(jnp.float32)
        ).astype(jnp.bfloat16)
        pair_copy(sub).wait_send()
        pair_copy(2 + sub).wait_send()
        cross_copy(sub).wait_send()
    for way in (0, 1):
        for hop in range(hops[way]):
            ring_copy(way, hop, hop == 0).wait_send()


def ring_project(product, weight, own):
    tokens = product.shape[0]
    peers = lax.axis_size("ctx")
    step = own.shape[1]
    width = weight.shape[1] // lax.axis_size("mp")
    chunks = 4
    box = (chunks, tokens // chunks, width)
    bf16, f32 = jnp.bfloat16, jnp.float32
    vmem = pl.BlockSpec(memory_space=pltpu.VMEM)
    return pl.pallas_call(
        functools.partial(ring_project_kernel, peers),
        in_specs=[vmem] * 3,
        out_specs=vmem,
        out_shape=jax.ShapeDtypeStruct((tokens, 2 * width), bf16),
        scratch_shapes=[pltpu.VMEM(box, bf16)] * 6
        + [pltpu.VMEM(box, f32)] * 2
        + [pltpu.VMEM((peers,) + own.shape, bf16)]
        + [pltpu.VMEM((4, tokens, step), bf16)] * 2
        + [pltpu.VMEM((2, tokens, step), bf16)] * 2
        + [pltpu.VMEM((4, tokens, step), f32)]
        + [
            pltpu.SemaphoreType.DMA((6, chunks)),
            pltpu.SemaphoreType.DMA((4, peers)),
            pltpu.SemaphoreType.DMA((4, 4)),
        ],
        compiler_params=pltpu.CompilerParams(
            collective_id=2, has_side_effects=True, vmem_limit_bytes=52 << 20
        ),
        name="ring_project",
    )(product, weight, own)


def cols(*lead):
    return pl.BlockSpec(lead + (LANES,), lambda i: (0,) * len(lead) + (i,))


def whole(shape):
    return pl.BlockSpec(shape, lambda i: (0,) * len(shape))


def local(q_in, k_in, v_in, short_filter, taps, residue, rate, out_weight):
    tokens, chans = q_in.shape
    block = taps.shape[0]
    modes = rate.shape[0]
    pieces = tokens // block
    fwd, rev, inv = [split_const(m) for m in dft_matrices(block)]
    grid = (chans // LANES,)
    f32, bf16 = jnp.float32, jnp.bfloat16
    lead = shifted(jnp.stack([q_in[-LEAD:], k_in[-LEAD:], v_in[-LEAD:]]), "ctx")
    filt_spec = cols(3, SHORT_LEN)
    params = pltpu.CompilerParams(vmem_limit_bytes=48 << 20)
    y_part, ends, state, tail = pl.pallas_call(
        local_kernel,
        grid=grid,
        in_specs=[
            cols(tokens), cols(tokens), cols(3, LEAD), filt_spec, cols(block), cols(modes),
            cols(modes), whole(fwd.shape), whole(rev.shape), whole(inv.shape),
        ],
        out_specs=[cols(tokens), cols(modes, pieces), cols(modes), cols(block)],
        out_shape=[
            jax.ShapeDtypeStruct((tokens, chans), f32),
            jax.ShapeDtypeStruct((modes, pieces, chans), f32),
            jax.ShapeDtypeStruct((modes, chans), f32),
            jax.ShapeDtypeStruct((block, chans), bf16),
        ],
        scratch_shapes=[
            pltpu.VMEM((LEAD + tokens, LANES), f32),
            pltpu.VMEM((LEAD + tokens, LANES), f32),
            pltpu.VMEM((tokens, LANES), f32),
        ],
        compiler_params=params,
        name="local_conv",
    )(k_in, v_in, lead, short_filter, taps, residue, rate, fwd, rev, inv)

    all_states, before = exchange(state, tail)
    gap = lax.axis_index("ctx") - 1 - jnp.arange(all_states.shape[0])
    spans = (jnp.maximum(gap, 0) * tokens).astype(f32)[:, None, None]
    carried = jnp.where((gap >= 0)[:, None, None], jnp.exp(-rate[None] * spans) * all_states, 0.0)
    start = jnp.sum(carried, axis=0)

    product = pl.pallas_call(
        finish_kernel,
        grid=grid,
        in_specs=[
            cols(tokens), cols(modes, pieces), cols(modes), cols(block), cols(tokens),
            cols(3, LEAD), filt_spec, cols(block), cols(modes), cols(modes),
            whole(fwd.shape), whole(inv.shape),
        ],
        out_specs=cols(tokens),
        out_shape=jax.ShapeDtypeStruct((tokens, chans), bf16),
        scratch_shapes=[
            pltpu.VMEM((LEAD + tokens, LANES), f32),
            pltpu.VMEM((modes, block, LANES), f32),
            pltpu.VMEM((pieces, modes, LANES), f32),
        ],
        compiler_params=params,
        name="finish_conv",
    )(y_part, ends, start, before, q_in, lead, short_filter, taps, residue, rate, fwd, inv)

    columns = out_weight.shape[1]
    peers, groups = lax.axis_size("ctx"), lax.axis_size("mp")
    if peers == 2 * groups and columns % 256 == 0:
        half = columns // 2
        early = lax.all_gather(out_weight[:, :half], "ctx", axis=1, tiled=True)
        return ring_project(product, early, out_weight[:, half:])
    return project(product, lax.all_gather(out_weight, "ctx", axis=1, tiled=True))


def solution(mesh):
    in_specs = (
        P("ctx", "mp"),
        P("ctx", "mp"),
        P("ctx", "mp"),
        P(None, None, "mp"),
        P(None, "mp"),
        P(None, "mp"),
        P(None, "mp"),
        P("mp", "ctx"),
    )
    out_specs = P("ctx", "mp")
    return jax.shard_map(local, mesh=mesh, in_specs=in_specs, out_specs=out_specs, check_vma=False)
```

```python
import functools

import jax
import jax.numpy as jnp
import numpy as np
from jax import lax
from jax.experimental import pallas as pl
from jax.experimental.pallas import tpu as pltpu
from jax.sharding import PartitionSpec as P

SHORT_LEN = 7
LANES = 128
LEAD = 8


def shifted(array, axis):
    peers = lax.axis_size(axis)
    return lax.ppermute(array, axis, [(i, i + 1) for i in range(peers - 1)])


def split_const(matrix):
    high = matrix.astype(jnp.bfloat16)
    low = (matrix - high.astype(np.float64)).astype(jnp.bfloat16)
    return jnp.asarray(np.stack([high, low]))


@functools.lru_cache
def dft_matrices(block):
    size = 2 * block
    freq = np.arange(block)[:, None]
    pos = np.arange(block)[None, :]
    angle = 2 * np.pi * ((freq * pos) % size) / size
    fwd = np.concatenate([np.cos(angle), -np.sin(angle)])
    fwd[block] = 1.0 - 2.0 * (np.arange(block) % 2)
    out_pos = block + np.arange(block)[:, None]
    freq = np.arange(block)[None, :]
    angle = 2 * np.pi * ((freq * out_pos) % size) / size
    real = 2 * np.cos(angle)
    imag = -2 * np.sin(angle)
    real[:, 0] = 1.0
    imag[:, 0] = 1.0 - 2.0 * (np.arange(block) % 2)
    inv = np.concatenate([real, imag], 1) / size
    return fwd, fwd[:, ::-1], inv


def mm(a, b):
    return jnp.dot(a, b, preferred_element_type=jnp.float32)


def mm_wide(pair, values):
    high = values.astype(jnp.bfloat16)
    low = (values - high.astype(jnp.float32)).astype(jnp.bfloat16)
    return mm(pair[0], high) + mm(pair[0], low) + mm(pair[1], high)


def spectrum_parts(spec, block, row0):
    real, imag = spec[:block], spec[block:]
    return real, jnp.where(row0, 0.0, imag), jnp.where(row0, imag, real)


def spectrum_mul(parts, spec, block):
    real, imag, cross = parts
    sr, si = spec[:block], spec[block:]
    return real * sr - imag * si, cross * si + imag * sr


def fill(scratch, lead_rows, signal):
    scratch[:LEAD] = lead_rows.astype(jnp.float32)
    scratch[LEAD:] = signal.astype(jnp.float32)


def short_taps(scratch, filt, start, block):
    total = filt[0:1] * scratch[LEAD + start : LEAD + start + block]
    for lag in range(1, SHORT_LEN):
        first = LEAD + start - lag
        total = total + filt[lag : lag + 1] * scratch[first : first + block]
    return total


def local_kernel(
    k_ref, v_ref, lead_ref, filt_ref, taps_ref, res_ref, rate_ref, fwd_ref, rev_ref, inv_ref,
    y_ref, ends_ref, state_ref, tail_ref, ks, vs, gs,
):
    block = taps_ref.shape[0]
    pieces = k_ref.shape[0] // block
    modes = rate_ref.shape[0]
    fill(ks, lead_ref[1], k_ref[...])
    fill(vs, lead_ref[2], v_ref[...])
    for b in range(pieces):
        gated = short_taps(ks, filt_ref[1], b * block, block) * short_taps(
            vs, filt_ref[2], b * block, block
        )
        gs[b * block : (b + 1) * block] = gated.astype(jnp.bfloat16).astype(jnp.float32)
    rows = lax.broadcasted_iota(jnp.int32, (block, LANES), 0)
    back = (block - 1 - rows).astype(jnp.float32)

    def one_mode(n, h_rev):
        rate = rate_ref[pl.ds(n, 1), :]
        decay = jnp.exp(-rate * back)
        for b in range(pieces):
            ends_ref[n, b : b + 1, :] = jnp.sum(
                decay * gs[b * block : (b + 1) * block], axis=0, keepdims=True
            )
        return h_rev + (res_ref[pl.ds(n, 1), :] * jnp.sqrt(2.0 * rate)) * decay

    h_rev = lax.fori_loop(
        0, modes, one_mode, jnp.zeros((block, LANES), jnp.float32), unroll=2
    )

    step = jnp.exp(-rate_ref[...] * float(block))
    state = ends_ref[:, 0, :]
    for b in range(1, pieces):
        state = step * state + ends_ref[:, b, :]
    state_ref[...] = state

    row0 = rows == 0
    sign = (1 - 2 * (rows % 2)).astype(jnp.float32)
    sign = jnp.concatenate([sign, sign], 0)
    taps_spec = mm_wide(fwd_ref, taps_ref[...])
    near_spec = sign * (taps_spec + mm_wide(rev_ref, h_rev))
    far = spectrum_parts(taps_spec, block, row0)
    near = spectrum_parts(near_spec, block, row0)
    previous = None
    for b in range(pieces):
        signal = gs[b * block : (b + 1) * block].astype(jnp.bfloat16)
        spec = mm(fwd_ref[0], signal) + mm(fwd_ref[1], signal)
        real, imag = spectrum_mul(near, spec, block)
        if previous is not None:
            more_real, more_imag = spectrum_mul(far, previous, block)
            real, imag = real + more_real, imag + more_imag
        y_ref[b * block : (b + 1) * block] = mm_wide(inv_ref, jnp.concatenate([real, imag], 0))
        previous = spec
        if b == pieces - 1:
            tail_ref[...] = signal


def finish_kernel(
    y_ref, ends_ref, start_ref, tail_ref, q_ref, lead_ref, filt_ref, taps_ref, res_ref, rate_ref,
    fwd_ref, inv_ref, out_ref, qs, lift, states,
):
    block = taps_ref.shape[0]
    pieces = q_ref.shape[0] // block
    modes = rate_ref.shape[0]
    fill(qs, lead_ref[0], q_ref[...])
    rows = lax.broadcasted_iota(jnp.int32, (block, LANES), 0)
    ahead = (rows + 1).astype(jnp.float32)
    for n in range(modes):
        rate = rate_ref[n : n + 1, :]
        lift[n] = (res_ref[n : n + 1, :] * jnp.sqrt(2.0 * rate)) * jnp.exp(-rate * ahead)
    step = jnp.exp(-rate_ref[...] * float(block))
    state = start_ref[...]
    states[0] = state
    for b in range(1, pieces):
        state = step * state + ends_ref[:, b - 1, :]
        states[b] = state
    taps_spec = mm_wide(fwd_ref, taps_ref[...])
    far = spectrum_parts(taps_spec, block, rows == 0)
    tail = tail_ref[...]
    spec = mm(fwd_ref[0], tail) + mm(fwd_ref[1], tail)
    halo = mm_wide(inv_ref, jnp.concatenate(spectrum_mul(far, spec, block), 0))
    for b in range(pieces):
        span = slice(b * block, (b + 1) * block)
        total = y_ref[span]
        if b == 0:
            total = total + halo
        for n in range(modes):
            total = total + lift[n] * states[b, n : n + 1, :]
        q_short = short_taps(qs, filt_ref[0], b * block, block).astype(jnp.bfloat16)
        long_conv = total.astype(jnp.bfloat16)
        out_ref[span] = (q_short.astype(jnp.float32) * long_conv.astype(jnp.float32)).astype(
            jnp.bfloat16
        )

MESH = pl.DeviceIdType.MESH


def exchange_kernel(peers, state_ref, tail_ref, all_ref, before_ref, send, recv, tail_sems):
    me = lax.axis_index("ctx")
    barrier = pltpu.get_barrier_semaphore()
    for hop in range(1, peers):
        pl.semaphore_signal(
            barrier, inc=1, device_id={"ctx": lax.rem(me + hop, peers)}, device_id_type=MESH
        )
    pl.semaphore_wait(barrier, peers - 1)

    def tail_copy(peer):
        return pltpu.make_async_remote_copy(
            src_ref=tail_ref, dst_ref=before_ref, send_sem=tail_sems.at[0],
            recv_sem=tail_sems.at[1], device_id={"ctx": peer}, device_id_type=MESH,
        )

    def state_copy(peer, slot, hop):
        return pltpu.make_async_remote_copy(
            src_ref=state_ref, dst_ref=all_ref.at[slot], send_sem=send.at[hop],
            recv_sem=recv.at[slot], device_id={"ctx": peer}, device_id_type=MESH,
        )

    @pl.when(me < peers - 1)
    def _():
        tail_copy(me + 1).start()

    for hop in range(1, peers):
        state_copy(lax.rem(me + hop, peers), me, hop).start()
    all_ref[me] = state_ref[...]

    @pl.when(me == 0)
    def _():
        before_ref[...] = jnp.zeros_like(before_ref)

    for hop in range(1, peers):
        source = lax.rem(me + hop, peers)
        state_copy(source, source, hop).wait_recv()
        state_copy(source, me, hop).wait_send()

    @pl.when(me > 0)
    def _():
        tail_copy(me).wait_recv()

    @pl.when(me < peers - 1)
    def _():
        tail_copy(me + 1).wait_send()


def exchange(state, tail):
    peers = lax.axis_size("ctx")
    vmem = pl.BlockSpec(memory_space=pltpu.VMEM)
    return pl.pallas_call(
        functools.partial(exchange_kernel, peers),
        in_specs=[vmem] * 2,
        out_specs=[vmem] * 2,
        out_shape=[
            jax.ShapeDtypeStruct((peers,) + state.shape, state.dtype),
            jax.ShapeDtypeStruct(tail.shape, tail.dtype),
        ],
        scratch_shapes=[
            pltpu.SemaphoreType.DMA((peers,)),
            pltpu.SemaphoreType.DMA((peers,)),
            pltpu.SemaphoreType.DMA((2,)),
        ],
        compiler_params=pltpu.CompilerParams(collective_id=0, has_side_effects=True),
        name="state_exchange",
    )(state, tail)


def project_kernel(
    prod_ref, w_ref, out_ref, near_out, near_in, far_out, far_in, mine_out, mine_in, hold, total,
    sems,
):
    me = lax.axis_index("mp")
    high, low = me // 2, lax.rem(me, 2)
    pair = high * 2 + (1 - low)
    across = (1 - high) * 2 + low
    chunks, rows, width = near_out.shape
    step = 256

    barrier = pltpu.get_barrier_semaphore()
    for peer in (pair, across):
        pl.semaphore_signal(barrier, inc=1, device_id={"mp": peer}, device_id_type=MESH)
    pl.semaphore_wait(barrier, 2)

    def copy(kind, t, source, target, peer):
        return pltpu.make_async_remote_copy(
            src_ref=source.at[t], dst_ref=target.at[t], send_sem=sems.at[2 * kind, t],
            recv_sem=sems.at[2 * kind + 1, t], device_id={"mp": peer}, device_id_type=MESH,
        )

    def near_copy(t):
        return copy(0, t, near_out, near_in, pair)

    def far_copy(t):
        return copy(1, t, far_out, far_in, across)

    def mine_copy(t):
        return copy(2, t, mine_out, mine_in, pair)

    def partial(t, owner, put):
        left = prod_ref[pl.ds(pl.multiple_of(t * rows, rows), rows), :]
        for col in range(0, width, step):
            first = pl.multiple_of(owner * width + col, step)
            put(col, mm(left, w_ref[:, pl.ds(first, step)]))

    def send_near(t):
        def put(col, value):
            near_out[t, :, col : col + step] = value.astype(jnp.bfloat16)

        partial(t, (1 - high) * 2 + (1 - low), put)
        near_copy(t).start()

        def keep(col, value):
            hold[t, :, col : col + step] = value

        partial(t, across, keep)

    def send_far(t):
        near_copy(t).wait_recv()
        far_out[t] = (hold[t] + near_in[t].astype(jnp.float32)).astype(jnp.bfloat16)
        far_copy(t).start()

    def first_pass(t, carry):
        send_near(t)

        @pl.when(t > 0)
        def _():
            send_far(t - 1)

        return carry

    lax.fori_loop(0, chunks, first_pass, 0)
    send_far(chunks - 1)

    def second_pass(t, carry):
        def put(col, value):
            mine_out[t, :, col : col + step] = value.astype(jnp.bfloat16)

        partial(t, pair, put)
        mine_copy(t).start()

        def keep(col, value):
            total[t, :, col : col + step] = value

        partial(t, me, keep)
        return carry

    lax.fori_loop(0, chunks, second_pass, 0)

    def finish(t, carry):
        mine_copy(t).wait_recv()
        far_copy(t).wait_recv()
        summed = total[t] + mine_in[t].astype(jnp.float32) + far_in[t].astype(jnp.float32)
        out_ref[pl.ds(pl.multiple_of(t * rows, rows), rows), :] = summed.astype(jnp.bfloat16)
        near_copy(t).wait_send()
        far_copy(t).wait_send()
        mine_copy(t).wait_send()
        return carry

    lax.fori_loop(0, chunks, finish, 0)


def project(product, weight):
    tokens = product.shape[0]
    width = weight.shape[1] // lax.axis_size("mp")
    chunks = 8
    box = (chunks, tokens // chunks, width)
    vmem = pl.BlockSpec(memory_space=pltpu.VMEM)
    return pl.pallas_call(
        project_kernel,
        in_specs=[vmem] * 2,
        out_specs=vmem,
        out_shape=jax.ShapeDtypeStruct((tokens, width), jnp.bfloat16),
        scratch_shapes=[pltpu.VMEM(box, jnp.bfloat16)] * 6
        + [pltpu.VMEM(box, jnp.float32)] * 2
        + [pltpu.SemaphoreType.DMA((6, chunks))],
        compiler_params=pltpu.CompilerParams(
            collective_id=1, has_side_effects=True, vmem_limit_bytes=48 << 20
        ),
        name="project",
    )(product, weight)


def ring_place(chip, count):
    odd = chip % 2
    return (chip // 2) * (1 - odd) + (count - 1 - chip // 2) * odd


def ring_chip(place, count):
    back = place // (count // 2)
    return 2 * place * (1 - back) + (2 * (count - 1 - place) + 1) * back


def ring_project_kernel(
    peers, prod_ref, w_ref, own_ref, out_ref, near_out, near_in, far_out, far_in, mine_out,
    mine_in, hold, total, ring, pair_out, pair_in, cross_out, cross_in, kept, sems, ring_sems,
    unit_sems,
):
    me = lax.axis_index("mp")
    high, low = me // 2, lax.rem(me, 2)
    pair = high * 2 + (1 - low)
    across = (1 - high) * 2 + low
    place = ring_place(lax.axis_index("ctx"), peers)
    chunks, rows, width = near_out.shape
    step = own_ref.shape[1]
    row_step = 256

    def neighbour(offset):
        return lax.rem(place + offset + peers, peers)

    ahead, behind = ring_chip(neighbour(1), peers), ring_chip(neighbour(-1), peers)
    barrier = pltpu.get_barrier_semaphore()
    for peer in (pair, across):
        pl.semaphore_signal(barrier, inc=1, device_id={"mp": peer}, device_id_type=MESH)
    for peer in (ahead, behind):
        pl.semaphore_signal(barrier, inc=1, device_id={"ctx": peer}, device_id_type=MESH)
    pl.semaphore_wait(barrier, 4)

    hops = peers // 2
    half = own_ref.shape[0] // 2

    def ring_span(way, hop):
        return pl.ds(way * half, half) if hop == hops - 1 else pl.ds(0, 2 * half)

    def ring_copy(way, hop, first):
        owner = ring_chip(neighbour(-hop if way == 0 else hop), peers)
        span = ring_span(way, hop)
        return pltpu.make_async_remote_copy(
            src_ref=own_ref if first else ring.at[owner, span], dst_ref=ring.at[owner, span],
            send_sem=ring_sems.at[2 * way, hop], recv_sem=ring_sems.at[2 * way + 1, hop],
            device_id={"ctx": behind if way else ahead}, device_id_type=MESH,
        )

    for way in (0, 1):
        ring_copy(way, 0, True).start()

    def copy(kind, t, source, target, peer):
        return pltpu.make_async_remote_copy(
            src_ref=source.at[t], dst_ref=target.at[t], send_sem=sems.at[2 * kind, t],
            recv_sem=sems.at[2 * kind + 1, t], device_id={"mp": peer}, device_id_type=MESH,
        )

    def near_copy(t):
        return copy(0, t, near_out, near_in, pair)

    def far_copy(t):
        return copy(1, t, far_out, far_in, across)

    def mine_copy(t):
        return copy(2, t, mine_out, mine_in, pair)

    def partial(t, owner, put):
        left = prod_ref[pl.ds(pl.multiple_of(t * rows, rows), rows), :]
        for col in range(0, width, step):
            first = pl.multiple_of(owner * width + col, step)
            put(col, mm(left, w_ref[:, pl.ds(first, step)]))

    def send_far(t):
        near_copy(t).wait_recv()
        far_out[t] = (hold[t] + near_in[t].astype(jnp.float32)).astype(jnp.bfloat16)
        far_copy(t).start()

    def first_pass(t, carry):
        def put(col, value):
            near_out[t, :, col : col + step] = value.astype(jnp.bfloat16)

        partial(t, (1 - high) * 2 + (1 - low), put)
        near_copy(t).start()

        def keep(col, value):
            hold[t, :, col : col + step] = value

        partial(t, across, keep)

        @pl.when(t > 0)
        def _():
            send_far(t - 1)

        return carry

    lax.fori_loop(0, chunks, first_pass, 0)
    send_far(chunks - 1)

    def second_pass(t, carry):
        def put(col, value):
            mine_out[t, :, col : col + step] = value.astype(jnp.bfloat16)

        partial(t, pair, put)
        mine_copy(t).start()

        def keep(col, value):
            total[t, :, col : col + step] = value

        partial(t, me, keep)
        return carry

    lax.fori_loop(0, chunks, second_pass, 0)

    def pair_copy(slot):
        return pltpu.make_async_remote_copy(
            src_ref=pair_out.at[slot], dst_ref=pair_in.at[slot], send_sem=unit_sems.at[0, slot],
            recv_sem=unit_sems.at[1, slot], device_id={"mp": pair}, device_id_type=MESH,
        )

    def cross_copy(slot):
        return pltpu.make_async_remote_copy(
            src_ref=cross_out.at[slot], dst_ref=cross_in.at[slot],
            send_sem=unit_sems.at[2, slot], recv_sem=unit_sems.at[3, slot],
            device_id={"mp": across}, device_id_type=MESH,
        )

    def unit(chip, first):
        owner, sub = chip // 2, lax.rem(chip, 2)
        gap = owner // 2 - high
        same = 1 - gap * gap
        slot = same * 2 + sub
        mine = lax.rem(owner, 2) == low

        def products(put):
            def body(r, carry):
                at = pl.ds(pl.multiple_of(r * row_step, row_step), row_step)
                right = own_ref[...] if first else ring[chip]
                put(at, mm(prod_ref[at, :], right))
                return carry

            lax.fori_loop(0, prod_ref.shape[0] // row_step, body, 0)

        @pl.when(jnp.logical_not(mine))
        def _():
            def put(at, value):
                pair_out[slot, at, :] = value.astype(jnp.bfloat16)

            products(put)
            pair_copy(slot).start()

        @pl.when(mine)
        def _():
            def put(at, value):
                kept[slot, at, :] = value

            products(put)

            @pl.when(same == 0)
            def _():
                pair_copy(slot).wait_recv()
                cross_out[sub] = (kept[slot] + pair_in[slot].astype(jnp.float32)).astype(
                    jnp.bfloat16
                )
                cross_copy(sub).start()

    unit(ring_chip(place, peers), True)

    def arrived(way, hop):
        return ring_chip(neighbour(-hop - 1 if way == 0 else hop + 1), peers)

    def finish(t, carry):
        mine_copy(t).wait_recv()
        far_copy(t).wait_recv()
        summed = total[t] + mine_in[t].astype(jnp.float32) + far_in[t].astype(jnp.float32)
        at = pl.ds(pl.multiple_of(t * rows, rows), rows)
        for part in range(width // step):
            out_ref[at, 2 * part * step : (2 * part + 1) * step] = summed[
                :, part * step : (part + 1) * step
            ].astype(jnp.bfloat16)
        near_copy(t).wait_send()
        far_copy(t).wait_send()
        mine_copy(t).wait_send()
        return carry

    for hop in range(hops):
        last = hop == hops - 1
        if last:
            lax.fori_loop(0, chunks, finish, 0)
        for way in (0, 1):
            span = ring_span(way, hop)
            pltpu.make_async_remote_copy(
                src_ref=own_ref.at[span], dst_ref=ring.at[arrived(way, hop), span],
                send_sem=ring_sems.at[2 * way, hop], recv_sem=ring_sems.at[2 * way + 1, hop],
                device_id={"ctx": behind if way else ahead}, device_id_type=MESH,
            ).wait_recv()
            if not last:
                ring_copy(way, hop + 1, False).start()
        for way in (0,) if last else (0, 1):
            unit(arrived(way, hop), False)

    for sub in range(2):
        pair_copy(2 + sub).wait_recv()
        cross_copy(sub).wait_recv()
        summed = kept[2 + sub] + pair_in[2 + sub].astype(jnp.float32)
        out_ref[:, (2 * sub + 1) * step : (2 * sub + 2) * step] = (
            summed + cross_in[sub].astype(jnp.float32)
        ).astype(jnp.bfloat16)
        pair_copy(sub).wait_send()
        pair_copy(2 + sub).wait_send()
        cross_copy(sub).wait_send()
    for way in (0, 1):
        for hop in range(hops):
            ring_copy(way, hop, hop == 0).wait_send()


def ring_project(product, weight, own):
    tokens = product.shape[0]
    peers = lax.axis_size("ctx")
    step = own.shape[1]
    width = weight.shape[1] // lax.axis_size("mp")
    chunks = 4
    box = (chunks, tokens // chunks, width)
    bf16, f32 = jnp.bfloat16, jnp.float32
    vmem = pl.BlockSpec(memory_space=pltpu.VMEM)
    return pl.pallas_call(
        functools.partial(ring_project_kernel, peers),
        in_specs=[vmem] * 3,
        out_specs=vmem,
        out_shape=jax.ShapeDtypeStruct((tokens, 2 * width), bf16),
        scratch_shapes=[pltpu.VMEM(box, bf16)] * 6
        + [pltpu.VMEM(box, f32)] * 2
        + [pltpu.VMEM((peers,) + own.shape, bf16)]
        + [pltpu.VMEM((4, tokens, step), bf16)] * 2
        + [pltpu.VMEM((2, tokens, step), bf16)] * 2
        + [pltpu.VMEM((4, tokens, step), f32)]
        + [
            pltpu.SemaphoreType.DMA((6, chunks)),
            pltpu.SemaphoreType.DMA((4, peers)),
            pltpu.SemaphoreType.DMA((4, 4)),
        ],
        compiler_params=pltpu.CompilerParams(
            collective_id=2, has_side_effects=True, vmem_limit_bytes=52 << 20
        ),
        name="ring_project",
    )(product, weight, own)


def cols(*lead):
    return pl.BlockSpec(lead + (LANES,), lambda i: (0,) * len(lead) + (i,))


def whole(shape):
    return pl.BlockSpec(shape, lambda i: (0,) * len(shape))


def local(q_in, k_in, v_in, short_filter, taps, residue, rate, out_weight):
    tokens, chans = q_in.shape
    block = taps.shape[0]
    modes = rate.shape[0]
    pieces = tokens // block
    fwd, rev, inv = [split_const(m) for m in dft_matrices(block)]
    grid = (chans // LANES,)
    f32, bf16 = jnp.float32, jnp.bfloat16
    lead = shifted(jnp.stack([q_in[-LEAD:], k_in[-LEAD:], v_in[-LEAD:]]), "ctx")
    filt_spec = cols(3, SHORT_LEN)
    params = pltpu.CompilerParams(vmem_limit_bytes=62 << 20)
    y_part, ends, state, tail = pl.pallas_call(
        local_kernel,
        grid=grid,
        in_specs=[
            cols(tokens), cols(tokens), cols(3, LEAD), filt_spec, cols(block), cols(modes),
            cols(modes), whole(fwd.shape), whole(rev.shape), whole(inv.shape),
        ],
        out_specs=[cols(tokens), cols(modes, pieces), cols(modes), cols(block)],
        out_shape=[
            jax.ShapeDtypeStruct((tokens, chans), f32),
            jax.ShapeDtypeStruct((modes, pieces, chans), f32),
            jax.ShapeDtypeStruct((modes, chans), f32),
            jax.ShapeDtypeStruct((block, chans), bf16),
        ],
        scratch_shapes=[
            pltpu.VMEM((LEAD + tokens, LANES), f32),
            pltpu.VMEM((LEAD + tokens, LANES), f32),
            pltpu.VMEM((tokens, LANES), f32),
        ],
        compiler_params=params,
        name="local_conv",
    )(k_in, v_in, lead, short_filter, taps, residue, rate, fwd, rev, inv)

    all_states, before = exchange(state, tail)
    gap = lax.axis_index("ctx") - 1 - jnp.arange(all_states.shape[0])
    spans = (jnp.maximum(gap, 0) * tokens).astype(f32)[:, None, None]
    carried = jnp.where((gap >= 0)[:, None, None], jnp.exp(-rate[None] * spans) * all_states, 0.0)
    start = jnp.sum(carried, axis=0)

    product = pl.pallas_call(
        finish_kernel,
        grid=grid,
        in_specs=[
            cols(tokens), cols(modes, pieces), cols(modes), cols(block), cols(tokens),
            cols(3, LEAD), filt_spec, cols(block), cols(modes), cols(modes),
            whole(fwd.shape), whole(inv.shape),
        ],
        out_specs=cols(tokens),
        out_shape=jax.ShapeDtypeStruct((tokens, chans), bf16),
        scratch_shapes=[
            pltpu.VMEM((LEAD + tokens, LANES), f32),
            pltpu.VMEM((modes, block, LANES), f32),
            pltpu.VMEM((pieces, modes, LANES), f32),
        ],
        compiler_params=params,
        name="finish_conv",
    )(y_part, ends, start, before, q_in, lead, short_filter, taps, residue, rate, fwd, inv)

    columns = out_weight.shape[1]
    peers, groups = lax.axis_size("ctx"), lax.axis_size("mp")
    if peers == 2 * groups and columns % 256 == 0:
        half = columns // 2
        early = lax.all_gather(out_weight[:, :half], "ctx", axis=1, tiled=True)
        return ring_project(product, early, out_weight[:, half:])
    return project(product, lax.all_gather(out_weight, "ctx", axis=1, tiled=True))


def solution(mesh):
    in_specs = (
        P("ctx", "mp"),
        P("ctx", "mp"),
        P("ctx", "mp"),
        P(None, None, "mp"),
        P(None, "mp"),
        P(None, "mp"),
        P(None, "mp"),
        P("mp", "ctx"),
    )
    out_specs = P("ctx", "mp")
    return jax.shard_map(local, mesh=mesh, in_specs=in_specs, out_specs=out_specs, check_vma=False)
```

```python
import functools

import jax
import jax.numpy as jnp
import numpy as np
from jax import lax
from jax.experimental import pallas as pl
from jax.experimental.pallas import tpu as pltpu
from jax.sharding import PartitionSpec as P

SHORT_LEN = 7
LANES = 128
LEAD = 8


def shifted(array, axis):
    peers = lax.axis_size(axis)
    return lax.ppermute(array, axis, [(i, i + 1) for i in range(peers - 1)])


def split_const(matrix):
    high = matrix.astype(jnp.bfloat16)
    low = (matrix - high.astype(np.float64)).astype(jnp.bfloat16)
    return jnp.asarray(np.stack([high, low]))


@functools.lru_cache
def dft_matrices(block):
    size = 2 * block
    freq = np.arange(block)[:, None]
    pos = np.arange(block)[None, :]
    angle = 2 * np.pi * ((freq * pos) % size) / size
    fwd = np.concatenate([np.cos(angle), -np.sin(angle)])
    fwd[block] = 1.0 - 2.0 * (np.arange(block) % 2)
    out_pos = block + np.arange(block)[:, None]
    freq = np.arange(block)[None, :]
    angle = 2 * np.pi * ((freq * out_pos) % size) / size
    real = 2 * np.cos(angle)
    imag = -2 * np.sin(angle)
    real[:, 0] = 1.0
    imag[:, 0] = 1.0 - 2.0 * (np.arange(block) % 2)
    inv = np.concatenate([real, imag], 1) / size
    return fwd, fwd[:, ::-1], inv


def mm(a, b):
    return jnp.dot(a, b, preferred_element_type=jnp.float32)


def mm_wide(pair, values):
    high = values.astype(jnp.bfloat16)
    low = (values - high.astype(jnp.float32)).astype(jnp.bfloat16)
    return mm(pair[0], high) + mm(pair[0], low) + mm(pair[1], high)


def spectrum_parts(spec, block, row0):
    real, imag = spec[:block], spec[block:]
    return real, jnp.where(row0, 0.0, imag), jnp.where(row0, imag, real)


def spectrum_mul(parts, spec, block):
    real, imag, cross = parts
    sr, si = spec[:block], spec[block:]
    return real * sr - imag * si, cross * si + imag * sr


def fill(scratch, lead_rows, signal):
    scratch[:LEAD] = lead_rows.astype(jnp.float32)
    scratch[LEAD:] = signal.astype(jnp.float32)


def short_taps(scratch, filt, start, block):
    total = filt[0:1] * scratch[LEAD + start : LEAD + start + block]
    for lag in range(1, SHORT_LEN):
        first = LEAD + start - lag
        total = total + filt[lag : lag + 1] * scratch[first : first + block]
    return total


def local_kernel(
    k_ref, v_ref, lead_ref, filt_ref, res_ref, rate_ref, gated_ref, h_rev_ref, ends_ref,
    state_ref, tail_ref, ks, vs, gs,
):
    block = h_rev_ref.shape[0]
    pieces = k_ref.shape[0] // block
    modes = rate_ref.shape[0]
    fill(ks, lead_ref[1], k_ref[...])
    fill(vs, lead_ref[2], v_ref[...])
    for b in range(pieces):
        gated = short_taps(ks, filt_ref[1], b * block, block) * short_taps(
            vs, filt_ref[2], b * block, block
        )
        rounded = gated.astype(jnp.bfloat16)
        gated_ref[b * block : (b + 1) * block] = rounded
        gs[b * block : (b + 1) * block] = rounded.astype(jnp.float32)
        if b == pieces - 1:
            tail_ref[...] = rounded
    rows = lax.broadcasted_iota(jnp.int32, (block, LANES), 0)
    back = (block - 1 - rows).astype(jnp.float32)

    def one_mode(n, h_rev):
        rate = rate_ref[pl.ds(n, 1), :]
        decay = jnp.exp(-rate * back)
        for b in range(pieces):
            ends_ref[n, b : b + 1, :] = jnp.sum(
                decay * gs[b * block : (b + 1) * block], axis=0, keepdims=True
            )
        return h_rev + (res_ref[pl.ds(n, 1), :] * jnp.sqrt(2.0 * rate)) * decay

    h_rev_ref[...] = lax.fori_loop(
        0, modes, one_mode, jnp.zeros((block, LANES), jnp.float32), unroll=2
    )

    step = jnp.exp(-rate_ref[...] * float(block))
    state = ends_ref[:, 0, :]
    for b in range(1, pieces):
        state = step * state + ends_ref[:, b, :]
    state_ref[...] = state


def block_kernel(
    peers, gated_ref, h_rev_ref, taps_ref, fwd_ref, rev_ref, inv_ref, states_ref, tail_ref,
    y_ref, all_ref, before_ref, landed, landed_tail, send, recv, tail_sems,
):
    index = pl.program_id(0)

    @pl.when(index == 0)
    def _():
        exchange_start(peers, states_ref, tail_ref, landed, landed_tail, send, recv, tail_sems)

    block = taps_ref.shape[0]
    pieces = gated_ref.shape[0] // block
    rows = lax.broadcasted_iota(jnp.int32, (block, LANES), 0)
    row0 = rows == 0
    sign = (1 - 2 * (rows % 2)).astype(jnp.float32)
    sign = jnp.concatenate([sign, sign], 0)
    taps_spec = mm_wide(fwd_ref, taps_ref[...])
    near_spec = sign * (taps_spec + mm_wide(rev_ref, h_rev_ref[...]))
    far = spectrum_parts(taps_spec, block, row0)
    near = spectrum_parts(near_spec, block, row0)
    previous = None
    for b in range(pieces):
        signal = gated_ref[b * block : (b + 1) * block]
        spec = mm(fwd_ref[0], signal) + mm(fwd_ref[1], signal)
        real, imag = spectrum_mul(near, spec, block)
        if previous is not None:
            more_real, more_imag = spectrum_mul(far, previous, block)
            real, imag = real + more_real, imag + more_imag
        y_ref[b * block : (b + 1) * block] = mm_wide(inv_ref, jnp.concatenate([real, imag], 0))
        previous = spec

    @pl.when(index == pl.num_programs(0) - 1)
    def _():
        exchange_finish(peers, states_ref, tail_ref, landed, landed_tail, send, recv, tail_sems)
        all_ref[...] = landed[...]
        before_ref[...] = landed_tail[...]


def finish_kernel(
    y_ref, ends_ref, start_ref, tail_ref, q_ref, lead_ref, filt_ref, taps_ref, res_ref, rate_ref,
    fwd_ref, inv_ref, out_ref, qs, lift, states,
):
    block = taps_ref.shape[0]
    pieces = q_ref.shape[0] // block
    modes = rate_ref.shape[0]
    fill(qs, lead_ref[0], q_ref[...])
    rows = lax.broadcasted_iota(jnp.int32, (block, LANES), 0)
    ahead = (rows + 1).astype(jnp.float32)
    for n in range(modes):
        rate = rate_ref[n : n + 1, :]
        lift[n] = (res_ref[n : n + 1, :] * jnp.sqrt(2.0 * rate)) * jnp.exp(-rate * ahead)
    step = jnp.exp(-rate_ref[...] * float(block))
    state = start_ref[...]
    states[0] = state
    for b in range(1, pieces):
        state = step * state + ends_ref[:, b - 1, :]
        states[b] = state
    taps_spec = mm_wide(fwd_ref, taps_ref[...])
    far = spectrum_parts(taps_spec, block, rows == 0)
    tail = tail_ref[...]
    spec = mm(fwd_ref[0], tail) + mm(fwd_ref[1], tail)
    halo = mm_wide(inv_ref, jnp.concatenate(spectrum_mul(far, spec, block), 0))
    for b in range(pieces):
        span = slice(b * block, (b + 1) * block)
        total = y_ref[span]
        if b == 0:
            total = total + halo
        for n in range(modes):
            total = total + lift[n] * states[b, n : n + 1, :]
        q_short = short_taps(qs, filt_ref[0], b * block, block).astype(jnp.bfloat16)
        long_conv = total.astype(jnp.bfloat16)
        out_ref[span] = (q_short.astype(jnp.float32) * long_conv.astype(jnp.float32)).astype(
            jnp.bfloat16
        )

MESH = pl.DeviceIdType.MESH


def tail_copy(peer, tail_ref, before_ref, tail_sems):
    return pltpu.make_async_remote_copy(
        src_ref=tail_ref, dst_ref=before_ref, send_sem=tail_sems.at[0],
        recv_sem=tail_sems.at[1], device_id={"ctx": peer}, device_id_type=MESH,
    )


def state_copy(peer, slot, hop, state_ref, all_ref, send, recv):
    return pltpu.make_async_remote_copy(
        src_ref=state_ref, dst_ref=all_ref.at[slot], send_sem=send.at[hop],
        recv_sem=recv.at[slot], device_id={"ctx": peer}, device_id_type=MESH,
    )


def exchange_start(peers, state_ref, tail_ref, all_ref, before_ref, send, recv, tail_sems):
    me = lax.axis_index("ctx")
    barrier = pltpu.get_barrier_semaphore()
    for hop in range(1, peers):
        pl.semaphore_signal(
            barrier, inc=1, device_id={"ctx": lax.rem(me + hop, peers)}, device_id_type=MESH
        )
    pl.semaphore_wait(barrier, peers - 1)

    @pl.when(me < peers - 1)
    def _():
        tail_copy(me + 1, tail_ref, before_ref, tail_sems).start()

    for hop in range(1, peers):
        state_copy(lax.rem(me + hop, peers), me, hop, state_ref, all_ref, send, recv).start()
    all_ref[me] = state_ref[...]

    @pl.when(me == 0)
    def _():
        before_ref[...] = jnp.zeros_like(before_ref)


def exchange_finish(peers, state_ref, tail_ref, all_ref, before_ref, send, recv, tail_sems):
    me = lax.axis_index("ctx")
    for hop in range(1, peers):
        source = lax.rem(me + hop, peers)
        state_copy(source, source, hop, state_ref, all_ref, send, recv).wait_recv()
        state_copy(source, me, hop, state_ref, all_ref, send, recv).wait_send()

    @pl.when(me > 0)
    def _():
        tail_copy(me, tail_ref, before_ref, tail_sems).wait_recv()

    @pl.when(me < peers - 1)
    def _():
        tail_copy(me + 1, tail_ref, before_ref, tail_sems).wait_send()


def project_kernel(
    prod_ref, w_ref, out_ref, near_out, near_in, far_out, far_in, mine_out, mine_in, hold, total,
    sems,
):
    me = lax.axis_index("mp")
    high, low = me // 2, lax.rem(me, 2)
    pair = high * 2 + (1 - low)
    across = (1 - high) * 2 + low
    chunks, rows, width = near_out.shape
    step = 256

    barrier = pltpu.get_barrier_semaphore()
    for peer in (pair, across):
        pl.semaphore_signal(barrier, inc=1, device_id={"mp": peer}, device_id_type=MESH)
    pl.semaphore_wait(barrier, 2)

    def copy(kind, t, source, target, peer):
        return pltpu.make_async_remote_copy(
            src_ref=source.at[t], dst_ref=target.at[t], send_sem=sems.at[2 * kind, t],
            recv_sem=sems.at[2 * kind + 1, t], device_id={"mp": peer}, device_id_type=MESH,
        )

    def near_copy(t):
        return copy(0, t, near_out, near_in, pair)

    def far_copy(t):
        return copy(1, t, far_out, far_in, across)

    def mine_copy(t):
        return copy(2, t, mine_out, mine_in, pair)

    def partial(t, owner, put):
        left = prod_ref[pl.ds(pl.multiple_of(t * rows, rows), rows), :]
        for col in range(0, width, step):
            first = pl.multiple_of(owner * width + col, step)
            put(col, mm(left, w_ref[:, pl.ds(first, step)]))

    def send_near(t):
        def put(col, value):
            near_out[t, :, col : col + step] = value.astype(jnp.bfloat16)

        partial(t, (1 - high) * 2 + (1 - low), put)
        near_copy(t).start()

        def keep(col, value):
            hold[t, :, col : col + step] = value

        partial(t, across, keep)

    def send_far(t):
        near_copy(t).wait_recv()
        far_out[t] = (hold[t] + near_in[t].astype(jnp.float32)).astype(jnp.bfloat16)
        far_copy(t).start()

    def first_pass(t, carry):
        send_near(t)

        @pl.when(t > 0)
        def _():
            send_far(t - 1)

        return carry

    lax.fori_loop(0, chunks, first_pass, 0)
    send_far(chunks - 1)

    def second_pass(t, carry):
        def put(col, value):
            mine_out[t, :, col : col + step] = value.astype(jnp.bfloat16)

        partial(t, pair, put)
        mine_copy(t).start()

        def keep(col, value):
            total[t, :, col : col + step] = value

        partial(t, me, keep)
        return carry

    lax.fori_loop(0, chunks, second_pass, 0)

    def finish(t, carry):
        mine_copy(t).wait_recv()
        far_copy(t).wait_recv()
        summed = total[t] + mine_in[t].astype(jnp.float32) + far_in[t].astype(jnp.float32)
        out_ref[pl.ds(pl.multiple_of(t * rows, rows), rows), :] = summed.astype(jnp.bfloat16)
        near_copy(t).wait_send()
        far_copy(t).wait_send()
        mine_copy(t).wait_send()
        return carry

    lax.fori_loop(0, chunks, finish, 0)


def project(product, weight):
    tokens = product.shape[0]
    width = weight.shape[1] // lax.axis_size("mp")
    chunks = 8
    box = (chunks, tokens // chunks, width)
    vmem = pl.BlockSpec(memory_space=pltpu.VMEM)
    return pl.pallas_call(
        project_kernel,
        in_specs=[vmem] * 2,
        out_specs=vmem,
        out_shape=jax.ShapeDtypeStruct((tokens, width), jnp.bfloat16),
        scratch_shapes=[pltpu.VMEM(box, jnp.bfloat16)] * 6
        + [pltpu.VMEM(box, jnp.float32)] * 2
        + [pltpu.SemaphoreType.DMA((6, chunks))],
        compiler_params=pltpu.CompilerParams(
            collective_id=1, has_side_effects=True, vmem_limit_bytes=48 << 20
        ),
        name="project",
    )(product, weight)


def ring_place(chip, count):
    odd = chip % 2
    return (chip // 2) * (1 - odd) + (count - 1 - chip // 2) * odd


def ring_chip(place, count):
    back = place // (count // 2)
    return 2 * place * (1 - back) + (2 * (count - 1 - place) + 1) * back


def ring_project_kernel(
    peers, prod_ref, w_ref, own_ref, out_ref, near_out, near_in, far_out, far_in, mine_out,
    mine_in, hold, total, ring, pair_out, pair_in, cross_out, cross_in, kept, sems, ring_sems,
    unit_sems,
):
    me = lax.axis_index("mp")
    high, low = me // 2, lax.rem(me, 2)
    pair = high * 2 + (1 - low)
    across = (1 - high) * 2 + low
    place = ring_place(lax.axis_index("ctx"), peers)
    chunks, rows, width = near_out.shape
    step = own_ref.shape[1]
    row_step = 256

    def neighbour(offset):
        return lax.rem(place + offset + peers, peers)

    ahead, behind = ring_chip(neighbour(1), peers), ring_chip(neighbour(-1), peers)
    barrier = pltpu.get_barrier_semaphore()
    for peer in (pair, across):
        pl.semaphore_signal(barrier, inc=1, device_id={"mp": peer}, device_id_type=MESH)
    for peer in (ahead, behind):
        pl.semaphore_signal(barrier, inc=1, device_id={"ctx": peer}, device_id_type=MESH)
    pl.semaphore_wait(barrier, 4)

    hops = peers // 2
    half = own_ref.shape[0] // 2

    def ring_span(way, hop):
        return pl.ds(way * half, half) if hop == hops - 1 else pl.ds(0, 2 * half)

    def ring_copy(way, hop, first):
        owner = ring_chip(neighbour(-hop if way == 0 else hop), peers)
        span = ring_span(way, hop)
        return pltpu.make_async_remote_copy(
            src_ref=own_ref if first else ring.at[owner, span], dst_ref=ring.at[owner, span],
            send_sem=ring_sems.at[2 * way, hop], recv_sem=ring_sems.at[2 * way + 1, hop],
            device_id={"ctx": behind if way else ahead}, device_id_type=MESH,
        )

    for way in (0, 1):
        ring_copy(way, 0, True).start()

    def copy(kind, t, source, target, peer):
        return pltpu.make_async_remote_copy(
            src_ref=source.at[t], dst_ref=target.at[t], send_sem=sems.at[2 * kind, t],
            recv_sem=sems.at[2 * kind + 1, t], device_id={"mp": peer}, device_id_type=MESH,
        )

    def near_copy(t):
        return copy(0, t, near_out, near_in, pair)

    def far_copy(t):
        return copy(1, t, far_out, far_in, across)

    def mine_copy(t):
        return copy(2, t, mine_out, mine_in, pair)

    def partial(t, owner, put):
        left = prod_ref[pl.ds(pl.multiple_of(t * rows, rows), rows), :]
        for col in range(0, width, step):
            first = pl.multiple_of(owner * width + col, step)
            put(col, mm(left, w_ref[:, pl.ds(first, step)]))

    def send_far(t):
        near_copy(t).wait_recv()
        far_out[t] = (hold[t] + near_in[t].astype(jnp.float32)).astype(jnp.bfloat16)
        far_copy(t).start()

    def first_pass(t, carry):
        def put(col, value):
            near_out[t, :, col : col + step] = value.astype(jnp.bfloat16)

        partial(t, (1 - high) * 2 + (1 - low), put)
        near_copy(t).start()

        def keep(col, value):
            hold[t, :, col : col + step] = value

        partial(t, across, keep)

        @pl.when(t > 0)
        def _():
            send_far(t - 1)

        return carry

    lax.fori_loop(0, chunks, first_pass, 0)
    send_far(chunks - 1)

    def second_pass(t, carry):
        def put(col, value):
            mine_out[t, :, col : col + step] = value.astype(jnp.bfloat16)

        partial(t, pair, put)
        mine_copy(t).start()

        def keep(col, value):
            total[t, :, col : col + step] = value

        partial(t, me, keep)
        return carry

    lax.fori_loop(0, chunks, second_pass, 0)

    def pair_copy(slot):
        return pltpu.make_async_remote_copy(
            src_ref=pair_out.at[slot], dst_ref=pair_in.at[slot], send_sem=unit_sems.at[0, slot],
            recv_sem=unit_sems.at[1, slot], device_id={"mp": pair}, device_id_type=MESH,
        )

    def cross_copy(slot):
        return pltpu.make_async_remote_copy(
            src_ref=cross_out.at[slot], dst_ref=cross_in.at[slot],
            send_sem=unit_sems.at[2, slot], recv_sem=unit_sems.at[3, slot],
            device_id={"mp": across}, device_id_type=MESH,
        )

    def unit(chip, first):
        owner, sub = chip // 2, lax.rem(chip, 2)
        gap = owner // 2 - high
        same = 1 - gap * gap
        slot = same * 2 + sub
        mine = lax.rem(owner, 2) == low

        def products(put):
            def body(r, carry):
                at = pl.ds(pl.multiple_of(r * row_step, row_step), row_step)
                right = own_ref[...] if first else ring[chip]
                put(at, mm(prod_ref[at, :], right))
                return carry

            lax.fori_loop(0, prod_ref.shape[0] // row_step, body, 0)

        @pl.when(jnp.logical_not(mine))
        def _():
            def put(at, value):
                pair_out[slot, at, :] = value.astype(jnp.bfloat16)

            products(put)
            pair_copy(slot).start()

        @pl.when(mine)
        def _():
            def put(at, value):
                kept[slot, at, :] = value

            products(put)

            @pl.when(same == 0)
            def _():
                pair_copy(slot).wait_recv()
                cross_out[sub] = (kept[slot] + pair_in[slot].astype(jnp.float32)).astype(
                    jnp.bfloat16
                )
                cross_copy(sub).start()

    unit(ring_chip(place, peers), True)

    def arrived(way, hop):
        return ring_chip(neighbour(-hop - 1 if way == 0 else hop + 1), peers)

    def finish(t, carry):
        mine_copy(t).wait_recv()
        far_copy(t).wait_recv()
        summed = total[t] + mine_in[t].astype(jnp.float32) + far_in[t].astype(jnp.float32)
        at = pl.ds(pl.multiple_of(t * rows, rows), rows)
        for part in range(width // step):
            out_ref[at, 2 * part * step : (2 * part + 1) * step] = summed[
                :, part * step : (part + 1) * step
            ].astype(jnp.bfloat16)
        near_copy(t).wait_send()
        far_copy(t).wait_send()
        mine_copy(t).wait_send()
        return carry

    for hop in range(hops):
        last = hop == hops - 1
        if last:
            lax.fori_loop(0, chunks, finish, 0)
        for way in (0, 1):
            span = ring_span(way, hop)
            pltpu.make_async_remote_copy(
                src_ref=own_ref.at[span], dst_ref=ring.at[arrived(way, hop), span],
                send_sem=ring_sems.at[2 * way, hop], recv_sem=ring_sems.at[2 * way + 1, hop],
                device_id={"ctx": behind if way else ahead}, device_id_type=MESH,
            ).wait_recv()
            if not last:
                ring_copy(way, hop + 1, False).start()
        for way in (0,) if last else (0, 1):
            unit(arrived(way, hop), False)

    for sub in range(2):
        pair_copy(2 + sub).wait_recv()
        cross_copy(sub).wait_recv()
        summed = kept[2 + sub] + pair_in[2 + sub].astype(jnp.float32)
        out_ref[:, (2 * sub + 1) * step : (2 * sub + 2) * step] = (
            summed + cross_in[sub].astype(jnp.float32)
        ).astype(jnp.bfloat16)
        pair_copy(sub).wait_send()
        pair_copy(2 + sub).wait_send()
        cross_copy(sub).wait_send()
    for way in (0, 1):
        for hop in range(hops):
            ring_copy(way, hop, hop == 0).wait_send()


def ring_project(product, weight, own):
    tokens = product.shape[0]
    peers = lax.axis_size("ctx")
    step = own.shape[1]
    width = weight.shape[1] // lax.axis_size("mp")
    chunks = 4
    box = (chunks, tokens // chunks, width)
    bf16, f32 = jnp.bfloat16, jnp.float32
    vmem = pl.BlockSpec(memory_space=pltpu.VMEM)
    return pl.pallas_call(
        functools.partial(ring_project_kernel, peers),
        in_specs=[vmem] * 3,
        out_specs=vmem,
        out_shape=jax.ShapeDtypeStruct((tokens, 2 * width), bf16),
        scratch_shapes=[pltpu.VMEM(box, bf16)] * 6
        + [pltpu.VMEM(box, f32)] * 2
        + [pltpu.VMEM((peers,) + own.shape, bf16)]
        + [pltpu.VMEM((4, tokens, step), bf16)] * 2
        + [pltpu.VMEM((2, tokens, step), bf16)] * 2
        + [pltpu.VMEM((4, tokens, step), f32)]
        + [
            pltpu.SemaphoreType.DMA((6, chunks)),
            pltpu.SemaphoreType.DMA((4, peers)),
            pltpu.SemaphoreType.DMA((4, 4)),
        ],
        compiler_params=pltpu.CompilerParams(
            collective_id=2, has_side_effects=True, vmem_limit_bytes=52 << 20
        ),
        name="ring_project",
    )(product, weight, own)


def cols(*lead):
    return pl.BlockSpec(lead + (LANES,), lambda i: (0,) * len(lead) + (i,))


def whole(shape):
    return pl.BlockSpec(shape, lambda i: (0,) * len(shape))


def local(q_in, k_in, v_in, short_filter, taps, residue, rate, out_weight):
    tokens, chans = q_in.shape
    block = taps.shape[0]
    modes = rate.shape[0]
    pieces = tokens // block
    fwd, rev, inv = [split_const(m) for m in dft_matrices(block)]
    grid = (chans // LANES,)
    f32, bf16 = jnp.float32, jnp.bfloat16
    lead = shifted(jnp.stack([q_in[-LEAD:], k_in[-LEAD:], v_in[-LEAD:]]), "ctx")
    filt_spec = cols(3, SHORT_LEN)
    params = pltpu.CompilerParams(vmem_limit_bytes=62 << 20)
    gated, h_rev, ends, state, tail = pl.pallas_call(
        local_kernel,
        grid=grid,
        in_specs=[
            cols(tokens), cols(tokens), cols(3, LEAD), filt_spec, cols(modes), cols(modes),
        ],
        out_specs=[cols(tokens), cols(block), cols(modes, pieces), cols(modes), cols(block)],
        out_shape=[
            jax.ShapeDtypeStruct((tokens, chans), bf16),
            jax.ShapeDtypeStruct((block, chans), f32),
            jax.ShapeDtypeStruct((modes, pieces, chans), f32),
            jax.ShapeDtypeStruct((modes, chans), f32),
            jax.ShapeDtypeStruct((block, chans), bf16),
        ],
        scratch_shapes=[
            pltpu.VMEM((LEAD + tokens, LANES), f32),
            pltpu.VMEM((LEAD + tokens, LANES), f32),
            pltpu.VMEM((tokens, LANES), f32),
        ],
        compiler_params=params,
        name="gate",
    )(k_in, v_in, lead, short_filter, residue, rate)

    peers = lax.axis_size("ctx")
    all_shape = (peers,) + state.shape
    y_part, all_states, before = pl.pallas_call(
        functools.partial(block_kernel, peers),
        grid=grid,
        in_specs=[
            cols(tokens), cols(block), cols(block), whole(fwd.shape), whole(rev.shape),
            whole(inv.shape), whole(state.shape), whole(tail.shape),
        ],
        out_specs=[cols(tokens), whole(all_shape), whole(tail.shape)],
        out_shape=[
            jax.ShapeDtypeStruct((tokens, chans), f32),
            jax.ShapeDtypeStruct(all_shape, f32),
            jax.ShapeDtypeStruct(tail.shape, bf16),
        ],
        scratch_shapes=[
            pltpu.VMEM(all_shape, f32),
            pltpu.VMEM(tail.shape, bf16),
            pltpu.SemaphoreType.DMA((peers,)),
            pltpu.SemaphoreType.DMA((peers,)),
            pltpu.SemaphoreType.DMA((2,)),
        ],
        compiler_params=pltpu.CompilerParams(
            collective_id=0, has_side_effects=True, vmem_limit_bytes=62 << 20
        ),
        name="block_conv",
    )(gated, h_rev, taps, fwd, rev, inv, state, tail)
    gap = lax.axis_index("ctx") - 1 - jnp.arange(all_states.shape[0])
    spans = (jnp.maximum(gap, 0) * tokens).astype(f32)[:, None, None]
    carried = jnp.where((gap >= 0)[:, None, None], jnp.exp(-rate[None] * spans) * all_states, 0.0)
    start = jnp.sum(carried, axis=0)

    product = pl.pallas_call(
        finish_kernel,
        grid=grid,
        in_specs=[
            cols(tokens), cols(modes, pieces), cols(modes), cols(block), cols(tokens),
            cols(3, LEAD), filt_spec, cols(block), cols(modes), cols(modes),
            whole(fwd.shape), whole(inv.shape),
        ],
        out_specs=cols(tokens),
        out_shape=jax.ShapeDtypeStruct((tokens, chans), bf16),
        scratch_shapes=[
            pltpu.VMEM((LEAD + tokens, LANES), f32),
            pltpu.VMEM((modes, block, LANES), f32),
            pltpu.VMEM((pieces, modes, LANES), f32),
        ],
        compiler_params=params,
        name="finish_conv",
    )(y_part, ends, start, before, q_in, lead, short_filter, taps, residue, rate, fwd, inv)

    columns = out_weight.shape[1]
    peers, groups = lax.axis_size("ctx"), lax.axis_size("mp")
    if peers == 2 * groups and columns % 256 == 0:
        half = columns // 2
        early = lax.all_gather(out_weight[:, :half], "ctx", axis=1, tiled=True)
        return ring_project(product, early, out_weight[:, half:])
    return project(product, lax.all_gather(out_weight, "ctx", axis=1, tiled=True))


def solution(mesh):
    in_specs = (
        P("ctx", "mp"),
        P("ctx", "mp"),
        P("ctx", "mp"),
        P(None, None, "mp"),
        P(None, "mp"),
        P(None, "mp"),
        P(None, "mp"),
        P("mp", "ctx"),
    )
    out_specs = P("ctx", "mp")
    return jax.shard_map(local, mesh=mesh, in_specs=in_specs, out_specs=out_specs, check_vma=False)
```
